256 devices in a mesh: slot: 8 (over y_lo, x), feat: 32 (over y_hi, z, core).
Axes of the slice: x: 4, y: 4 (y_hi: 2, y_lo: 2; y = y_hi * 2 + y_lo), z: 8, core: 2. Of those that a mesh axis runs over, the one named last changes fastest.
Arguments:
- acts_in: bfloat16 [3, 256, 2304], P(None, None, 'slot'), may hold values from -6 to 6
- acts_out: bfloat16 [3, 256, 2304], P(None, None, 'slot'), may hold values from -6 to 6
- enc_weight: bfloat16 [3, 2304, 16384], P(None, 'slot', 'feat'), may hold values from -0.125 to 0.125
- enc_bias: float32 [3, 16384], P(None, 'feat'), may hold values from -3 to 3
- dec_weight: bfloat16 [6, 16384, 2304], P(None, 'feat', 'slot'), may hold values from -0.046875 to 0.046875
- dec_bias: float32 [3, 2304], P(None, 'slot'), may hold values from -3 to 3
Outputs:
- enc_grad: float32 [3, 2304, 16384], P(None, 'slot', 'feat')
- enc_bias_grad: float32 [3, 16384], P(None, 'feat')
- dec_grad: float32 [6, 16384, 2304], P(None, 'feat', 'slot')
- mse: float32 [], replicated
The draws below stay inside these ranges and needn't reach their ends.
All inputs are finite; a program needn't handle non-finite values.
Results may differ from the reference program's by a relative error of at most 0.0095.
Values may be sent and summed in bfloat16 or wider, within the bound.
No kernel may reach another device: no remote copies, remote signals or barrier semaphores. Data moves between devices by JAX's collectives and lax.ppermute only.
A program may use at most 64 MiB of HBM per device.

```python
import jax
import jax.numpy as jnp
from jax import lax

D = 2304
F = 16384
L = 3
TOKENS = 256
PAIRS = 6


def block_scale(own_key, shape, split, smallest, high):
    factor_of = 1.0
    for axis_at, shards_of in split:
        steps = jax.random.uniform(jax.random.fold_in(jax.random.fold_in(own_key, 6), axis_at), (shards_of,), jnp.float32, smallest / len(split), high / len(split))
        factor_of = factor_of * jnp.repeat(jnp.exp(steps), shape[axis_at] // shards_of).reshape((-1,) + (1,) * (len(shape) - 1 - axis_at))
    return factor_of


def scatter_about(rng, dims, spread, most, cuts=(), kind=jnp.bfloat16):
    entries = spread * jax.random.normal(rng, dims, jnp.float32)
    if cuts:
        entries = entries * block_scale(rng, dims, cuts, -0.22, 0.18)
    return jnp.clip(entries, -most, most).astype(kind)


def setup_inputs(seed: int = 0) -> dict:
    key_list = jax.random.split(jax.random.key(seed), 7)
    return {
        "acts_in": scatter_about(key_list[0], (L, TOKENS, D), 1.0, 6.0, ((2, 8),)),
        "acts_out": scatter_about(key_list[1], (L, TOKENS, D), 1.0, 6.0, ((2, 8),)),
        "enc_weight": scatter_about(key_list[2], (L, D, F), D ** -0.5, 0.125, ((1, 8), (2, 32))),
        "enc_bias": scatter_about(key_list[3], (L, F), 0.5, 3.0, ((1, 32),), jnp.float32),
        "dec_weight": scatter_about(key_list[4], (PAIRS, F, D), F ** -0.5, 0.046875, ((1, 32), (2, 8))),
        "dec_bias": scatter_about(key_list[5], (L, D), 0.5, 3.0, ((1, 8),), jnp.float32),
    }


def pair_number(src_layer, dst_layer):
    return src_layer * L - src_layer * (src_layer - 1) // 2 + (dst_layer - src_layer)


def reference(acts_in, acts_out, enc_weight, enc_bias, dec_weight, dec_bias):
    features = []
    slopes = []
    for src_layer in range(L):
        preact = jnp.dot(acts_in[src_layer], enc_weight[src_layer], preferred_element_type=jnp.float32) + enc_bias[src_layer]
        features.append(jnp.maximum(preact, 0.0).astype(jnp.bfloat16))
        slopes.append(jnp.where(preact > 0, 1.0, 0.0).astype(jnp.bfloat16))
    errors = []
    squared = jnp.zeros((), jnp.float32)
    for dst_layer in range(L):
        rebuilt = jnp.zeros((TOKENS, D), jnp.float32)
        for src_layer in range(dst_layer + 1):
            rebuilt = rebuilt + jnp.dot(features[src_layer], dec_weight[pair_number(src_layer, dst_layer)], preferred_element_type=jnp.float32)
        error_full = rebuilt + dec_bias[dst_layer] - acts_out[dst_layer].astype(jnp.float32)
        squared = squared + jnp.sum(error_full * error_full)
        errors.append(error_full.astype(jnp.bfloat16))
    mse = squared / (L * TOKENS * D)
    dec_grads = []
    for src_layer in range(L):
        for dst_layer in range(src_layer, L):
            dec_grads.append(lax.dot_general(features[src_layer], errors[dst_layer], (((0,), (0,)), ((), ())), preferred_element_type=jnp.float32))
    enc_grads = []
    bias_grads = []
    for src_layer in range(L):
        upstream = jnp.zeros((TOKENS, F), jnp.float32)
        for dst_layer in range(src_layer, L):
            upstream = upstream + lax.dot_general(errors[dst_layer], dec_weight[pair_number(src_layer, dst_layer)], (((1,), (1,)), ((), ())), preferred_element_type=jnp.float32)
        delta = upstream * slopes[src_layer].astype(jnp.float32)
        bias_grads.append(jnp.sum(delta, axis=0))
        enc_grads.append(lax.dot_general(acts_in[src_layer], delta.astype(jnp.bfloat16), (((0,), (0,)), ((), ())), preferred_element_type=jnp.float32))
    return jnp.stack(enc_grads), jnp.stack(bias_grads), jnp.stack(dec_grads), mse
```

```python
import jax
import jax.numpy as jnp
from jax import lax
from jax.sharding import Mesh
from jax.sharding import PartitionSpec as P

D = 2304
SLOT = ("slot_0", "slot_1")
FEAT = ("feat_0", "feat_1", "feat_2")
CHIPS = ("feat_0", "feat_1")
CORE = "feat_2"


def exchange(tiles, axis):
    return lax.all_to_all(tiles, axis, split_axis=0, concat_axis=0, tiled=True)


def sent_to_all(x, axis):
    return exchange(jnp.broadcast_to(x[None], (lax.axis_size(axis), *x.shape)), axis)


def local(acts_in, acts_out, enc_weight, enc_bias, dec_weight, dec_bias):
    layers, tokens, width_dev = acts_in.shape
    feature_dev = enc_weight.shape[2]
    pair_list = [(a, b) for a in range(layers) for b in range(a, layers)]
    slots = lax.axis_size(SLOT)
    chips = lax.axis_size(CHIPS)
    core = lax.axis_index(CORE)
    f32, bf16 = jnp.float32, jnp.bfloat16

    def feats(x, a):
        return x[:, a * feature_dev : (a + 1) * feature_dev]

    def width(x, b):
        return x[:, b * width_dev : (b + 1) * width_dev]

    preact = jnp.concatenate(
        [jnp.dot(acts_in[a], enc_weight[a], preferred_element_type=f32) for a in range(layers)], axis=1
    )
    arrived = exchange(preact.reshape(slots, tokens // slots, -1), SLOT)
    own_preact = arrived.sum(axis=0) + enc_bias.reshape(1, -1)
    own_features = jnp.maximum(own_preact, 0.0).astype(bf16)
    features = sent_to_all(own_features, SLOT).reshape(tokens, -1)

    pieces = []
    for b in range(layers):
        summed = jnp.zeros((tokens, width_dev), f32)
        for a in range(b + 1):
            summed = summed + jnp.dot(
                feats(features, a), dec_weight[pair_list.index((a, b))], preferred_element_type=f32
            )
        pieces.append(summed)
    partial = jnp.concatenate(pieces, axis=1)
    half = tokens // 2
    theirs = lax.dynamic_slice_in_dim(partial, (1 - core) * half, half, 0).astype(bf16)
    mine = lax.dynamic_slice_in_dim(partial, core * half, half, 0)
    chip_sum = (mine + lax.ppermute(theirs, CORE, [(0, 1), (1, 0)]).astype(f32)).astype(bf16)
    portion = half // chips
    rebuilt = exchange(chip_sum.reshape(chips, portion, -1), CHIPS).astype(f32).sum(axis=0)
    offset = core * half + lax.axis_index(CHIPS) * portion
    target = lax.dynamic_slice_in_dim(acts_out, offset, portion, 1)
    target = jnp.transpose(target, (1, 0, 2)).reshape(portion, -1).astype(f32)
    own_error = (rebuilt + dec_bias.reshape(1, -1) - target).astype(bf16)
    half_error = sent_to_all(own_error, CHIPS).reshape(half, -1)
    error = lax.all_gather(half_error, CORE, axis=0, tiled=True)

    wide = error.astype(f32)
    squared = jnp.sum(wide * wide)
    coarse = lax.reduce_precision(squared, 8, 7)
    fine = lax.reduce_precision(squared - coarse, 8, 7)
    lane = lax.broadcasted_iota(jnp.int32, (tokens, 128), 1)
    extra = jnp.where(lane == 0, coarse, jnp.where(lane == 1, fine, 0.0))

    partials = []
    for a in range(layers):
        summed = jnp.zeros((tokens, feature_dev), f32)
        for b in range(a, layers):
            summed = summed + lax.dot_general(
                width(error, b),
                dec_weight[pair_list.index((a, b))],
                (((1,), (1,)), ((), ())),
                preferred_element_type=f32,
            )
        partials.append(summed)
    sent = jnp.concatenate([*partials, extra], axis=1).astype(bf16)
    total = exchange(sent.reshape(slots, tokens // slots, -1), SLOT).astype(f32).sum(axis=0)
    mse = (total[0, layers * feature_dev] + total[0, layers * feature_dev + 1]) / (layers * tokens * D)
    own_delta = jnp.where(own_features > 0, total[:, : layers * feature_dev], 0.0).astype(bf16)
    delta = sent_to_all(own_delta, SLOT).reshape(tokens, -1)

    dec_grads = [
        lax.dot_general(
            feats(features, a), width(error, b), (((0,), (0,)), ((), ())), preferred_element_type=f32
        )
        for a, b in pair_list
    ]
    bias_grad = jnp.sum(delta.astype(f32), axis=0).reshape(layers, feature_dev)
    enc_grads = [
        lax.dot_general(
            acts_in[a], feats(delta, a), (((0,), (0,)), ((), ())), preferred_element_type=f32
        )
        for a in range(layers)
    ]
    return (jnp.stack(enc_grads), bias_grad, jnp.stack(dec_grads), mse)


def solution(mesh):
    split = Mesh(mesh.devices.reshape(2, 4, 2, 8, 2), (*SLOT, *FEAT))
    in_specs = (
        P(None, None, SLOT),
        P(None, None, SLOT),
        P(None, SLOT, FEAT),
        P(None, FEAT),
        P(None, FEAT, SLOT),
        P(None, SLOT),
    )
    out_specs = (P(None, SLOT, FEAT), P(None, FEAT), P(None, FEAT, SLOT), P())
    return jax.shard_map(local, mesh=split, in_specs=in_specs, out_specs=out_specs, check_vma=False)
```

```python
import functools

import jax
import jax.numpy as jnp
from jax import lax
from jax.experimental import pallas as pl
from jax.experimental.pallas import tpu as pltpu
from jax.sharding import Mesh
from jax.sharding import PartitionSpec as P

D = 2304
SLOT = ("slot_0", "slot_1")
FEAT = ("feat_0", "feat_1", "feat_2")
CHIPS = ("feat_0", "feat_1")
CORE = "feat_2"
LANES = 128
VMEM = 16 * 2**20
F32 = jnp.float32
BF16 = jnp.bfloat16


def exchange(tiles, axis):
    return lax.all_to_all(tiles, axis, split_axis=0, concat_axis=0, tiled=True)


def sent_to_all(x, axis):
    return exchange(jnp.broadcast_to(x[None], (lax.axis_size(axis), *x.shape)), axis)


def pair_number(a, b, layers):
    return a * layers - a * (a - 1) // 2 + (b - a)


def contract(x, y, x_dim, y_dim):
    return lax.dot_general(x, y, (((x_dim,), (y_dim,)), ((), ())), preferred_element_type=F32)


def encode_kernel(acts_ref, weight_ref, out_ref):
    out_ref[...] = contract(acts_ref[0], weight_ref[0], 0, 0)


def encode(acts_t, enc_weight):
    layers, width, tokens = acts_t.shape
    feature_dev = enc_weight.shape[2]
    return pl.pallas_call(
        encode_kernel,
        grid=(layers,),
        in_specs=[
            pl.BlockSpec((1, width, tokens), lambda a: (a, 0, 0)),
            pl.BlockSpec((1, width, feature_dev), lambda a: (a, 0, 0)),
        ],
        out_specs=pl.BlockSpec((tokens, feature_dev), lambda a: (0, a)),
        out_shape=jax.ShapeDtypeStruct((tokens, layers * feature_dev), F32),
        name="encode",
    )(acts_t, enc_weight)


def decode_kernel(layers, core_ref, features_ref, weight_ref, theirs_ref, mine_ref):
    feature_dev = weight_ref.shape[2]
    width = weight_ref.shape[1]
    half = theirs_ref.shape[0]
    core = core_ref[0]
    for ref, side in ((theirs_ref, 1 - core), (mine_ref, core)):
        rows = pl.ds(pl.multiple_of(side * half, half), half)
        for b in range(layers):
            total = None
            for a in range(b + 1):
                term = contract(
                    features_ref[rows, a * feature_dev : (a + 1) * feature_dev],
                    weight_ref[pair_number(a, b, layers)],
                    1,
                    1,
                )
                total = term if total is None else total + term
            ref[:, b * width : (b + 1) * width] = total.astype(ref.dtype)


def decode(core, features, dec_t, layers):
    tokens = features.shape[0]
    shape = (tokens // 2, layers * dec_t.shape[1])
    vmem = pl.BlockSpec(memory_space=pltpu.VMEM)
    return pl.pallas_call(
        functools.partial(decode_kernel, layers),
        in_specs=[pl.BlockSpec(memory_space=pltpu.SMEM), vmem, vmem],
        out_specs=[vmem, vmem],
        out_shape=[jax.ShapeDtypeStruct(shape, BF16), jax.ShapeDtypeStruct(shape, F32)],
        compiler_params=pltpu.CompilerParams(vmem_limit_bytes=VMEM),
        name="decode",
    )(core, features, dec_t)


def upstream_kernel(layers, error_ref, weight_ref, out_ref):
    tokens = error_ref.shape[0]
    width, feature_dev = weight_ref.shape[1:]
    for a in range(layers):
        total = None
        for b in range(a, layers):
            term = contract(
                error_ref[:, b * width : (b + 1) * width], weight_ref[pair_number(a, b, layers)], 1, 0
            )
            total = term if total is None else total + term
        out_ref[:, a * feature_dev : (a + 1) * feature_dev] = total.astype(BF16)
    wide = error_ref[...].astype(F32)
    squared = jnp.sum(wide * wide)
    coarse = squared.astype(BF16).astype(F32)
    fine = squared - coarse
    lane = lax.broadcasted_iota(jnp.int32, (tokens, LANES), 1)
    extra = jnp.where(lane == 0, coarse, jnp.where(lane == 1, fine, 0.0))
    out_ref[:, layers * feature_dev :] = extra.astype(BF16)


def upstream(error, dec_t, layers):
    tokens = error.shape[0]
    vmem = pl.BlockSpec(memory_space=pltpu.VMEM)
    return pl.pallas_call(
        functools.partial(upstream_kernel, layers),
        in_specs=[vmem, vmem],
        out_specs=vmem,
        out_shape=jax.ShapeDtypeStruct((tokens, layers * dec_t.shape[2] + LANES), BF16),
        compiler_params=pltpu.CompilerParams(vmem_limit_bytes=VMEM),
        name="upstream",
    )(error, dec_t)


def encoder_grad_kernel(acts_ref, delta_ref, grad_ref, bias_ref):
    delta = delta_ref[...]
    grad_ref[0] = contract(acts_ref[0], delta, 1, 0)
    bias_ref[0] = jnp.sum(delta.astype(F32), axis=0, keepdims=True)


def encoder_grad(acts_t, delta):
    layers, width, tokens = acts_t.shape
    feature_dev = delta.shape[1] // layers
    grad, bias = pl.pallas_call(
        encoder_grad_kernel,
        grid=(layers,),
        in_specs=[
            pl.BlockSpec((1, width, tokens), lambda a: (a, 0, 0)),
            pl.BlockSpec((tokens, feature_dev), lambda a: (0, a)),
        ],
        out_specs=[
            pl.BlockSpec((1, width, feature_dev), lambda a: (a, 0, 0)),
            pl.BlockSpec((1, 1, feature_dev), lambda a: (a, 0, 0)),
        ],
        out_shape=[
            jax.ShapeDtypeStruct((layers, width, feature_dev), F32),
            jax.ShapeDtypeStruct((layers, 1, feature_dev), F32),
        ],
        compiler_params=pltpu.CompilerParams(vmem_limit_bytes=VMEM),
        name="encoder_grad",
    )(acts_t, delta)
    return grad, bias.reshape(layers, feature_dev)


def local(acts_in, acts_out, enc_weight, enc_bias, dec_weight, dec_bias):
    layers, tokens, width_dev = acts_in.shape
    feature_dev = enc_weight.shape[2]
    pair_list = [(a, b) for a in range(layers) for b in range(a, layers)]
    slots = lax.axis_size(SLOT)
    chips = lax.axis_size(CHIPS)
    core = lax.axis_index(CORE)
    acts_t = jnp.transpose(acts_in, (0, 2, 1))
    dec_t = jnp.transpose(dec_weight, (0, 2, 1))

    def feats(x, a):
        return x[:, a * feature_dev : (a + 1) * feature_dev]

    def width(x, b):
        return x[:, b * width_dev : (b + 1) * width_dev]

    preact = encode(acts_t, enc_weight)
    arrived = exchange(preact.reshape(slots, tokens // slots, -1), SLOT)
    own_preact = arrived.sum(axis=0) + enc_bias.reshape(1, -1)
    own_features = jnp.maximum(own_preact, 0.0).astype(BF16)
    features = sent_to_all(own_features, SLOT).reshape(tokens, -1)

    theirs, mine = decode(core.reshape(1), features, dec_t, layers)
    chip_sum = (mine + lax.ppermute(theirs, CORE, [(0, 1), (1, 0)]).astype(F32)).astype(BF16)
    half = tokens // 2
    portion = half // chips
    rebuilt = exchange(chip_sum.reshape(chips, portion, -1), CHIPS).astype(F32).sum(axis=0)
    offset = core * half + lax.axis_index(CHIPS) * portion
    target = lax.dynamic_slice_in_dim(acts_out, offset, portion, 1)
    target = jnp.transpose(target, (1, 0, 2)).reshape(portion, -1).astype(F32)
    own_error = (rebuilt + dec_bias.reshape(1, -1) - target).astype(BF16)
    half_error = sent_to_all(own_error, CHIPS).reshape(half, -1)
    error = lax.all_gather(half_error, CORE, axis=0, tiled=True)

    sent = upstream(error, dec_t, layers)
    total = exchange(sent.reshape(slots, tokens // slots, -1), SLOT).astype(F32).sum(axis=0)
    mse = (total[0, layers * feature_dev] + total[0, layers * feature_dev + 1]) / (layers * tokens * D)
    own_delta = jnp.where(own_features > 0, total[:, : layers * feature_dev], 0.0).astype(BF16)
    delta = sent_to_all(own_delta, SLOT).reshape(tokens, -1)

    dec_grads = [contract(feats(features, a), width(error, b), 0, 0) for a, b in pair_list]
    enc_grad, bias_grad = encoder_grad(acts_t, delta)
    return (enc_grad, bias_grad, jnp.stack(dec_grads), mse)


def solution(mesh):
    split = Mesh(mesh.devices.reshape(2, 4, 2, 8, 2), (*SLOT, *FEAT))
    in_specs = (
        P(None, None, SLOT),
        P(None, None, SLOT),
        P(None, SLOT, FEAT),
        P(None, FEAT),
        P(None, FEAT, SLOT),
        P(None, SLOT),
    )
    out_specs = (P(None, SLOT, FEAT), P(None, FEAT), P(None, FEAT, SLOT), P())
    return jax.shard_map(local, mesh=split, in_specs=in_specs, out_specs=out_specs, check_vma=False)
```

```python
import functools

import jax
import jax.numpy as jnp
from jax import lax
from jax.experimental import pallas as pl
from jax.experimental.pallas import tpu as pltpu
from jax.sharding import Mesh
from jax.sharding import PartitionSpec as P

D = 2304
SLOT = ("slot_0", "slot_1")
FEAT = ("feat_0", "feat_1", "feat_2")
CHIPS = ("feat_0", "feat_1")
CORE = "feat_2"
LANES = 128
VMEM = 16 * 2**20
F32 = jnp.float32
BF16 = jnp.bfloat16


def exchange(tiles, axis):
    return lax.all_to_all(tiles, axis, split_axis=0, concat_axis=0, tiled=True)


def sent_to_all(x, axis):
    return exchange(jnp.broadcast_to(x[None], (lax.axis_size(axis), *x.shape)), axis)


def pair_number(a, b, layers):
    return a * layers - a * (a - 1) // 2 + (b - a)


def contract(x, y, x_dim, y_dim):
    return lax.dot_general(x, y, (((x_dim,), (y_dim,)), ((), ())), preferred_element_type=F32)


def encode_kernel(acts_ref, weight_ref, out_ref, rounded_ref):
    preact = contract(acts_ref[0], weight_ref[0], 0, 0)
    out_ref[...] = preact
    rounded_ref[...] = preact.astype(BF16)


def encode(acts_t, enc_weight):
    layers, width, tokens = acts_t.shape
    feature_dev = enc_weight.shape[2]
    return pl.pallas_call(
        encode_kernel,
        grid=(layers,),
        in_specs=[
            pl.BlockSpec((1, width, tokens), lambda a: (a, 0, 0)),
            pl.BlockSpec((1, width, feature_dev), lambda a: (a, 0, 0)),
        ],
        out_specs=[pl.BlockSpec((tokens, feature_dev), lambda a: (0, a))] * 2,
        out_shape=[jax.ShapeDtypeStruct((tokens, layers * feature_dev), kind) for kind in (F32, BF16)],
        name="encode",
    )(acts_t, enc_weight)


def decode_kernel(layers, core_ref, features_ref, weight_ref, theirs_ref, mine_ref):
    feature_dev = weight_ref.shape[2]
    width = weight_ref.shape[1]
    half = theirs_ref.shape[0]
    core = core_ref[0]
    for ref, side in ((theirs_ref, 1 - core), (mine_ref, core)):
        rows = pl.ds(pl.multiple_of(side * half, half), half)
        for b in range(layers):
            total = None
            for a in range(b + 1):
                term = contract(
                    features_ref[rows, a * feature_dev : (a + 1) * feature_dev],
                    weight_ref[pair_number(a, b, layers)],
                    1,
                    1,
                )
                total = term if total is None else total + term
            ref[:, b * width : (b + 1) * width] = total.astype(ref.dtype)


def decode(core, features, dec_t, layers):
    tokens = features.shape[0]
    shape = (tokens // 2, layers * dec_t.shape[1])
    vmem = pl.BlockSpec(memory_space=pltpu.VMEM)
    return pl.pallas_call(
        functools.partial(decode_kernel, layers),
        in_specs=[pl.BlockSpec(memory_space=pltpu.SMEM), vmem, vmem],
        out_specs=[vmem, vmem],
        out_shape=[jax.ShapeDtypeStruct(shape, BF16), jax.ShapeDtypeStruct(shape, F32)],
        compiler_params=pltpu.CompilerParams(vmem_limit_bytes=VMEM),
        name="decode",
    )(core, features, dec_t)


def upstream_kernel(layers, error_ref, weight_ref, out_ref):
    tokens = error_ref.shape[0]
    width, feature_dev = weight_ref.shape[1:]
    for a in range(layers):
        total = None
        for b in range(a, layers):
            term = contract(
                error_ref[:, b * width : (b + 1) * width], weight_ref[pair_number(a, b, layers)], 1, 0
            )
            total = term if total is None else total + term
        out_ref[:, a * feature_dev : (a + 1) * feature_dev] = total.astype(BF16)
    wide = error_ref[...].astype(F32)
    squared = jnp.sum(wide * wide)
    coarse = squared.astype(BF16).astype(F32)
    fine = squared - coarse
    lane = lax.broadcasted_iota(jnp.int32, (tokens, LANES), 1)
    extra = jnp.where(lane == 0, coarse, jnp.where(lane == 1, fine, 0.0))
    out_ref[:, layers * feature_dev :] = extra.astype(BF16)


def upstream(error, dec_t, layers):
    tokens = error.shape[0]
    vmem = pl.BlockSpec(memory_space=pltpu.VMEM)
    return pl.pallas_call(
        functools.partial(upstream_kernel, layers),
        in_specs=[vmem, vmem],
        out_specs=vmem,
        out_shape=jax.ShapeDtypeStruct((tokens, layers * dec_t.shape[2] + LANES), BF16),
        compiler_params=pltpu.CompilerParams(vmem_limit_bytes=VMEM),
        name="upstream",
    )(error, dec_t)


def encoder_grad_kernel(acts_ref, delta_ref, grad_ref, bias_ref):
    delta = delta_ref[...]
    grad_ref[0] = contract(acts_ref[0], delta, 1, 0)
    bias_ref[0] = jnp.sum(delta.astype(F32), axis=0, keepdims=True)


def encoder_grad(acts_t, delta):
    layers, width, tokens = acts_t.shape
    feature_dev = delta.shape[1] // layers
    grad, bias = pl.pallas_call(
        encoder_grad_kernel,
        grid=(layers,),
        in_specs=[
            pl.BlockSpec((1, width, tokens), lambda a: (a, 0, 0)),
            pl.BlockSpec((tokens, feature_dev), lambda a: (0, a)),
        ],
        out_specs=[
            pl.BlockSpec((1, width, feature_dev), lambda a: (a, 0, 0)),
            pl.BlockSpec((1, 1, feature_dev), lambda a: (a, 0, 0)),
        ],
        out_shape=[
            jax.ShapeDtypeStruct((layers, width, feature_dev), F32),
            jax.ShapeDtypeStruct((layers, 1, feature_dev), F32),
        ],
        compiler_params=pltpu.CompilerParams(vmem_limit_bytes=VMEM),
        name="encoder_grad",
    )(acts_t, delta)
    return grad, bias.reshape(layers, feature_dev)


def local(acts_in, acts_out, enc_weight, enc_bias, dec_weight, dec_bias):
    layers, tokens, width_dev = acts_in.shape
    feature_dev = enc_weight.shape[2]
    pair_list = [(a, b) for a in range(layers) for b in range(a, layers)]
    slots = lax.axis_size(SLOT)
    chips = lax.axis_size(CHIPS)
    core = lax.axis_index(CORE)
    acts_t = jnp.transpose(acts_in, (0, 2, 1))
    dec_t = jnp.transpose(dec_weight, (0, 2, 1))

    def feats(x, a):
        return x[:, a * feature_dev : (a + 1) * feature_dev]

    def width(x, b):
        return x[:, b * width_dev : (b + 1) * width_dev]

    bias_row = enc_bias.reshape(1, -1)
    preact, rounded = encode(acts_t, enc_weight)
    arrived = exchange(rounded.reshape(slots, tokens // slots, -1), SLOT)
    own_preact = arrived.astype(F32).sum(axis=0) + bias_row
    own_features = jnp.maximum(own_preact, 0.0).astype(BF16)
    features = sent_to_all(own_features, SLOT).reshape(tokens, -1)
    features, preact = lax.optimization_barrier((features, preact))
    slope = lax.psum_scatter(preact, SLOT, scatter_dimension=0, tiled=True) + bias_row > 0

    theirs, mine = decode(core.reshape(1), features, dec_t, layers)
    chip_sum = (mine + lax.ppermute(theirs, CORE, [(0, 1), (1, 0)]).astype(F32)).astype(BF16)
    half = tokens // 2
    portion = half // chips
    rebuilt = exchange(chip_sum.reshape(chips, portion, -1), CHIPS).astype(F32).sum(axis=0)
    offset = core * half + lax.axis_index(CHIPS) * portion
    target = lax.dynamic_slice_in_dim(acts_out, offset, portion, 1)
    target = jnp.transpose(target, (1, 0, 2)).reshape(portion, -1).astype(F32)
    own_error = (rebuilt + dec_bias.reshape(1, -1) - target).astype(BF16)
    half_error = sent_to_all(own_error, CHIPS).reshape(half, -1)
    error = lax.all_gather(half_error, CORE, axis=0, tiled=True)

    sent = upstream(error, dec_t, layers)
    total = exchange(sent.reshape(slots, tokens // slots, -1), SLOT).astype(F32).sum(axis=0)
    mse = (total[0, layers * feature_dev] + total[0, layers * feature_dev + 1]) / (layers * tokens * D)
    own_delta = jnp.where(slope, total[:, : layers * feature_dev], 0.0).astype(BF16)
    delta = sent_to_all(own_delta, SLOT).reshape(tokens, -1)

    dec_grads = [contract(feats(features, a), width(error, b), 0, 0) for a, b in pair_list]
    enc_grad, bias_grad = encoder_grad(acts_t, delta)
    return (enc_grad, bias_grad, jnp.stack(dec_grads), mse)


def solution(mesh):
    split = Mesh(mesh.devices.reshape(2, 4, 2, 8, 2), (*SLOT, *FEAT))
    in_specs = (
        P(None, None, SLOT),
        P(None, None, SLOT),
        P(None, SLOT, FEAT),
        P(None, FEAT),
        P(None, FEAT, SLOT),
        P(None, SLOT),
    )
    out_specs = (P(None, SLOT, FEAT), P(None, FEAT), P(None, FEAT, SLOT), P())
    return jax.shard_map(local, mesh=split, in_specs=in_specs, out_specs=out_specs, check_vma=False)
```

```python
import functools

import jax
import jax.numpy as jnp
from jax import lax
from jax.experimental import pallas as pl
from jax.experimental.pallas import tpu as pltpu
from jax.sharding import Mesh
from jax.sharding import PartitionSpec as P

D = 2304
SLOT = ("slot_0", "slot_1")
FEAT = ("feat_0", "feat_1", "feat_2")
CHIPS = ("feat_0", "feat_1")
CORE = "feat_2"
LANES = 128
VMEM = 16 * 2**20
SPAN = 173.2868
ABOVE = 1.0078125
TINY = 1e-30
F32 = jnp.float32
BF16 = jnp.bfloat16


def exchange(tiles, axis):
    return lax.all_to_all(tiles, axis, split_axis=0, concat_axis=0, tiled=True)


def sent_to_all(x, axis):
    return exchange(jnp.broadcast_to(x[None], (lax.axis_size(axis), *x.shape)), axis)


def pair_number(a, b, layers):
    return a * layers - a * (a - 1) // 2 + (b - a)


def contract(x, y, x_dim, y_dim):
    return lax.dot_general(x, y, (((x_dim,), (y_dim,)), ((), ())), preferred_element_type=F32)


def start(copies):
    for copy in copies:
        copy.start()
    return copies


def finish(copies):
    for copy in copies:
        copy.wait()


def encode_kernel(acts_hbm, weight_hbm, out_hbm, acts_ref, weight_ref, held_ref, acts_sems, weight_sems, out_sems):
    layers = acts_ref.shape[0]
    feature_dev = weight_ref.shape[2]
    tokens = held_ref.shape[0]
    arriving = [
        start(
            [
                pltpu.make_async_copy(acts_hbm.at[a], acts_ref.at[a], acts_sems.at[a]),
                pltpu.make_async_copy(weight_hbm.at[a], weight_ref.at[a], weight_sems.at[a]),
            ]
        )
        for a in range(layers)
    ]
    leaving = []

    def send(step, columns):
        copy = pltpu.make_async_copy(held_ref.at[:, columns], out_hbm.at[:, columns], out_sems.at[step])
        leaving.extend(start([copy]))

    lane = lax.broadcasted_iota(jnp.int32, (tokens, LANES), 1)
    scales = jnp.zeros((tokens, LANES), F32)
    for a in range(layers):
        finish(arriving[a])
        preact = contract(acts_ref[a], weight_ref[a], 0, 0)
        size = jnp.abs(preact)
        largest = jnp.maximum(jnp.max(size, axis=1, keepdims=True), TINY)
        scale = (largest * ABOVE).astype(BF16).astype(F32)
        code = jnp.exp(jnp.sqrt(size * (1.0 / scale)) * SPAN - SPAN / 2)
        columns = pl.ds(a * feature_dev, feature_dev)
        held_ref[:, columns] = jnp.where(preact < 0, -code, code).astype(BF16)
        send(a, columns)
        scales = jnp.where(lane == a, scale, scales)
    columns = pl.ds(layers * feature_dev, LANES)
    held_ref[:, columns] = scales.astype(BF16)
    send(layers, columns)
    finish(leaving)


def encode(acts_t, enc_weight):
    layers, width, tokens = acts_t.shape
    feature_dev = enc_weight.shape[2]
    shape = (tokens, layers * feature_dev + LANES)
    anywhere = pl.BlockSpec(memory_space=pl.ANY)
    return pl.pallas_call(
        encode_kernel,
        in_specs=[anywhere, anywhere],
        out_specs=anywhere,
        out_shape=jax.ShapeDtypeStruct(shape, BF16),
        scratch_shapes=[
            pltpu.VMEM(acts_t.shape, BF16),
            pltpu.VMEM(enc_weight.shape, BF16),
            pltpu.VMEM(shape, BF16),
            pltpu.SemaphoreType.DMA((layers,)),
            pltpu.SemaphoreType.DMA((layers,)),
            pltpu.SemaphoreType.DMA((layers + 1,)),
        ],
        name="encode",
    )(acts_t, enc_weight)


def features_kernel(arrived_hbm, bias_ref, own_ref, out_hbm, arrived_ref, in_sems, out_sems):
    slots, rows, _ = arrived_ref.shape
    layers, feature_dev = bias_ref.shape
    arriving = start(
        [pltpu.make_async_copy(arrived_hbm.at[k], arrived_ref.at[k], in_sems.at[k]) for k in range(slots)]
    )
    totals = [jnp.broadcast_to(bias_ref[a : a + 1, :], (rows, feature_dev)) for a in range(layers)]
    for k in range(slots):
        arriving[k].wait()
        scales = arrived_ref[k, :, layers * feature_dev :].astype(F32)
        for a in range(layers):
            code = arrived_ref[k, :, a * feature_dev : (a + 1) * feature_dev].astype(F32)
            root = jnp.log(jnp.abs(code)) * (1.0 / SPAN) + 0.5
            size = root * root * scales[:, a : a + 1]
            totals[a] = totals[a] + jnp.where(code < 0, -size, size)
    for a in range(layers):
        own_ref[:, a * feature_dev : (a + 1) * feature_dev] = jnp.maximum(totals[a], 0.0).astype(BF16)
    finish(start([pltpu.make_async_copy(own_ref, out_hbm.at[k], out_sems.at[k]) for k in range(slots)]))


def own_features_of(arrived, enc_bias):
    slots, rows, _ = arrived.shape
    own = (rows, enc_bias.size)
    anywhere = pl.BlockSpec(memory_space=pl.ANY)
    vmem = pl.BlockSpec(memory_space=pltpu.VMEM)
    return pl.pallas_call(
        features_kernel,
        in_specs=[anywhere, vmem],
        out_specs=[vmem, anywhere],
        out_shape=[jax.ShapeDtypeStruct(own, BF16), jax.ShapeDtypeStruct((slots, *own), BF16)],
        scratch_shapes=[
            pltpu.VMEM(arrived.shape, BF16),
            pltpu.SemaphoreType.DMA((slots,)),
            pltpu.SemaphoreType.DMA((slots,)),
        ],
        name="own_features",
    )(arrived, enc_bias)


def delta_kernel(share, arrived_hbm, features_ref, mse_ref, out_hbm, arrived_ref, own_ref, in_sems, out_sems):
    slots = arrived_ref.shape[0]
    columns = features_ref.shape[1]
    arriving = start(
        [pltpu.make_async_copy(arrived_hbm.at[k], arrived_ref.at[k], in_sems.at[k]) for k in range(slots)]
    )
    arriving[0].wait()
    total = arrived_ref[0].astype(F32)
    for k in range(1, slots):
        arriving[k].wait()
        total = total + arrived_ref[k].astype(F32)
    own_ref[...] = jnp.where(features_ref[...] > 0, total[:, :columns], 0.0).astype(BF16)
    leaving = start([pltpu.make_async_copy(own_ref, out_hbm.at[k], out_sems.at[k]) for k in range(slots)])
    mse_ref[0, 0] = jnp.sum(total[:1, columns:]) * share
    finish(leaving)


def own_delta_of(arrived, own_features, share):
    slots = arrived.shape[0]
    own = own_features.shape
    anywhere = pl.BlockSpec(memory_space=pl.ANY)
    return pl.pallas_call(
        functools.partial(delta_kernel, share),
        in_specs=[anywhere, pl.BlockSpec(memory_space=pltpu.VMEM)],
        out_specs=[pl.BlockSpec(memory_space=pltpu.SMEM), anywhere],
        out_shape=[jax.ShapeDtypeStruct((1, 1), F32), jax.ShapeDtypeStruct((slots, *own), BF16)],
        scratch_shapes=[
            pltpu.VMEM(arrived.shape, BF16),
            pltpu.VMEM(own, BF16),
            pltpu.SemaphoreType.DMA((slots,)),
            pltpu.SemaphoreType.DMA((slots,)),
        ],
        name="own_delta",
    )(arrived, own_features)


def decode_kernel(layers, core_ref, features_ref, weight_ref, theirs_ref, mine_ref):
    feature_dev = weight_ref.shape[2]
    width = weight_ref.shape[1]
    half = theirs_ref.shape[0]
    core = core_ref[0]
    for ref, side in ((theirs_ref, 1 - core), (mine_ref, core)):
        rows = pl.ds(pl.multiple_of(side * half, half), half)
        for b in range(layers):
            total = None
            for a in range(b + 1):
                term = contract(
                    features_ref[rows, a * feature_dev : (a + 1) * feature_dev],
                    weight_ref[pair_number(a, b, layers)],
                    1,
                    1,
                )
                total = term if total is None else total + term
            ref[:, b * width : (b + 1) * width] = total.astype(ref.dtype)


def decode(core, features, dec_t, layers):
    tokens = features.shape[0]
    shape = (tokens // 2, layers * dec_t.shape[1])
    vmem = pl.BlockSpec(memory_space=pltpu.VMEM)
    return pl.pallas_call(
        functools.partial(decode_kernel, layers),
        in_specs=[pl.BlockSpec(memory_space=pltpu.SMEM), vmem, vmem],
        out_specs=[vmem, vmem],
        out_shape=[jax.ShapeDtypeStruct(shape, BF16), jax.ShapeDtypeStruct(shape, F32)],
        compiler_params=pltpu.CompilerParams(vmem_limit_bytes=VMEM),
        name="decode",
    )(core, features, dec_t)


def upstream_kernel(layers, error_ref, weight_ref, out_ref):
    tokens = error_ref.shape[0]
    width, feature_dev = weight_ref.shape[1:]
    for a in range(layers):
        total = None
        for b in range(a, layers):
            term = contract(
                error_ref[:, b * width : (b + 1) * width], weight_ref[pair_number(a, b, layers)], 1, 0
            )
            total = term if total is None else total + term
        out_ref[:, a * feature_dev : (a + 1) * feature_dev] = total.astype(BF16)
    wide = error_ref[...].astype(F32)
    squared = jnp.sum(wide * wide)
    coarse = squared.astype(BF16).astype(F32)
    fine = squared - coarse
    lane = lax.broadcasted_iota(jnp.int32, (tokens, LANES), 1)
    extra = jnp.where(lane == 0, coarse, jnp.where(lane == 1, fine, 0.0))
    out_ref[:, layers * feature_dev :] = extra.astype(BF16)


def upstream(error, dec_t, layers):
    tokens = error.shape[0]
    vmem = pl.BlockSpec(memory_space=pltpu.VMEM)
    return pl.pallas_call(
        functools.partial(upstream_kernel, layers),
        in_specs=[vmem, vmem],
        out_specs=vmem,
        out_shape=jax.ShapeDtypeStruct((tokens, layers * dec_t.shape[2] + LANES), BF16),
        compiler_params=pltpu.CompilerParams(vmem_limit_bytes=VMEM),
        name="upstream",
    )(error, dec_t)


def encoder_grad_kernel(acts_ref, delta_ref, grad_ref, bias_ref):
    delta = delta_ref[...]
    grad_ref[0] = contract(acts_ref[0], delta, 1, 0)
    bias_ref[pl.ds(pl.program_id(0), 1), :] = jnp.sum(delta.astype(F32), axis=0, keepdims=True)


def encoder_grad(acts_t, delta):
    layers, width, tokens = acts_t.shape
    feature_dev = delta.shape[1] // layers
    return pl.pallas_call(
        encoder_grad_kernel,
        grid=(layers,),
        in_specs=[
            pl.BlockSpec((1, width, tokens), lambda a: (a, 0, 0)),
            pl.BlockSpec((tokens, feature_dev), lambda a: (0, a)),
        ],
        out_specs=[
            pl.BlockSpec((1, width, feature_dev), lambda a: (a, 0, 0)),
            pl.BlockSpec((layers, feature_dev), lambda a: (0, 0)),
        ],
        out_shape=[
            jax.ShapeDtypeStruct((layers, width, feature_dev), F32),
            jax.ShapeDtypeStruct((layers, feature_dev), F32),
        ],
        compiler_params=pltpu.CompilerParams(vmem_limit_bytes=VMEM),
        name="encoder_grad",
    )(acts_t, delta)


def local(acts_in, acts_out, enc_weight, enc_bias, dec_weight, dec_bias):
    layers, tokens, width_dev = acts_in.shape
    feature_dev = enc_weight.shape[2]
    pair_list = [(a, b) for a in range(layers) for b in range(a, layers)]
    slots = lax.axis_size(SLOT)
    chips = lax.axis_size(CHIPS)
    core = lax.axis_index(CORE)
    acts_t = jnp.transpose(acts_in, (0, 2, 1))
    dec_t = jnp.transpose(dec_weight, (0, 2, 1))

    def feats(x, a):
        return x[:, a * feature_dev : (a + 1) * feature_dev]

    def width(x, b):
        return x[:, b * width_dev : (b + 1) * width_dev]

    sent = encode(acts_t, enc_weight)
    arrived = exchange(sent.reshape(slots, tokens // slots, -1), SLOT)
    own_features, copies = own_features_of(arrived, enc_bias)
    features = exchange(copies, SLOT).reshape(tokens, -1)

    theirs, mine = decode(core.reshape(1), features, dec_t, layers)
    chip_sum = (mine + lax.ppermute(theirs, CORE, [(0, 1), (1, 0)]).astype(F32)).astype(BF16)
    half = tokens // 2
    portion = half // chips
    rebuilt = exchange(chip_sum.reshape(chips, portion, -1), CHIPS).astype(F32).sum(axis=0)
    offset = core * half + lax.axis_index(CHIPS) * portion
    target = lax.dynamic_slice_in_dim(acts_out, offset, portion, 1)
    target = jnp.transpose(target, (1, 0, 2)).reshape(portion, -1).astype(F32)
    own_error = (rebuilt + dec_bias.reshape(1, -1) - target).astype(BF16)
    half_error = sent_to_all(own_error, CHIPS).reshape(half, -1)
    error = lax.all_gather(half_error, CORE, axis=0, tiled=True)

    sent = upstream(error, dec_t, layers)
    arrived = exchange(sent.reshape(slots, tokens // slots, -1), SLOT)
    mse, copies = own_delta_of(arrived, own_features, 1.0 / (layers * tokens * D))
    delta = exchange(copies, SLOT).reshape(tokens, -1)

    dec_grads = [contract(feats(features, a), width(error, b), 0, 0) for a, b in pair_list]
    enc_grad, bias_grad = encoder_grad(acts_t, delta)
    return (enc_grad, bias_grad, jnp.stack(dec_grads), mse.reshape(()))


def solution(mesh):
    split = Mesh(mesh.devices.reshape(2, 4, 2, 8, 2), (*SLOT, *FEAT))
    in_specs = (
        P(None, None, SLOT),
        P(None, None, SLOT),
        P(None, SLOT, FEAT),
        P(None, FEAT),
        P(None, FEAT, SLOT),
        P(None, SLOT),
    )
    out_specs = (P(None, SLOT, FEAT), P(None, FEAT), P(None, FEAT, SLOT), P())
    return jax.shard_map(local, mesh=split, in_specs=in_specs, out_specs=out_specs, check_vma=False)
```

```python
import functools

import jax
import jax.numpy as jnp
from jax import lax
from jax.experimental import pallas as pl
from jax.experimental.pallas import tpu as pltpu
from jax.sharding import Mesh
from jax.sharding import PartitionSpec as P

D = 2304
SLOT = ("slot_0", "slot_1")
FEAT = ("feat_0", "feat_1", "feat_2")
CHIPS = ("feat_0", "feat_1")
CORE = "feat_2"
LANES = 128
VMEM = 16 * 2**20
OCTAVES = 250.0
ABOVE = 1.0078125
TINY = 1e-30
LEAST = 1e-12
F32 = jnp.float32
BF16 = jnp.bfloat16


def exchange(tiles, axis):
    return lax.all_to_all(tiles, axis, split_axis=0, concat_axis=0, tiled=True)


def sent_to_all(x, axis):
    return exchange(jnp.broadcast_to(x[None], (lax.axis_size(axis), *x.shape)), axis)


def pair_number(a, b, layers):
    return a * layers - a * (a - 1) // 2 + (b - a)


def contract(x, y, x_dim, y_dim):
    return lax.dot_general(x, y, (((x_dim,), (y_dim,)), ((), ())), preferred_element_type=F32)


def encode_kernel(acts_ref, weight_ref, out_ref):
    layers = acts_ref.shape[0]
    tokens = out_ref.shape[0]
    feature_dev = weight_ref.shape[2]
    lane = lax.broadcasted_iota(jnp.int32, (tokens, LANES), 1)
    scales = jnp.zeros((tokens, LANES), F32)
    for a in range(layers):
        preact = contract(acts_ref[a], weight_ref[a], 0, 0)
        size = jnp.abs(preact)
        largest = jnp.maximum(jnp.max(size, axis=1, keepdims=True), TINY)
        scale = (largest * ABOVE).astype(BF16).astype(F32)
        square = jnp.maximum(size * (1.0 / scale), LEAST)
        code = jnp.exp2(square * lax.rsqrt(square) * OCTAVES - OCTAVES / 2)
        out_ref[:, a * feature_dev : (a + 1) * feature_dev] = jnp.where(preact < 0, -code, code).astype(BF16)
        scales = jnp.where(lane == a, scale, scales)
    out_ref[:, layers * feature_dev :] = scales.astype(BF16)


def on_chip(kernel, name, args, out_shape, scratch_shapes=()):
    vmem = pl.BlockSpec(memory_space=pltpu.VMEM)
    smem = pl.BlockSpec(memory_space=pltpu.SMEM)
    return pl.pallas_call(
        kernel,
        in_specs=[smem if arg.dtype == jnp.int32 else vmem for arg in args],
        out_specs=jax.tree.map(lambda _: vmem, out_shape),
        out_shape=out_shape,
        scratch_shapes=scratch_shapes,
        compiler_params=pltpu.CompilerParams(vmem_limit_bytes=VMEM),
        name=name,
    )(*args)


def encode(acts_t, enc_weight):
    layers, _, tokens = acts_t.shape
    shape = (tokens, layers * enc_weight.shape[2] + LANES)
    return on_chip(encode_kernel, "encode", (acts_t, enc_weight), jax.ShapeDtypeStruct(shape, BF16))


def features_kernel(arrived_ref, bias_ref, own_ref):
    slots, rows, _ = arrived_ref.shape
    layers, feature_dev = bias_ref.shape
    totals = [jnp.broadcast_to(bias_ref[a : a + 1, :], (rows, feature_dev)) for a in range(layers)]
    for k in range(slots):
        scales = arrived_ref[k, :, layers * feature_dev :].astype(F32)
        for a in range(layers):
            code = arrived_ref[k, :, a * feature_dev : (a + 1) * feature_dev].astype(F32)
            root = jnp.log2(jnp.abs(code)) * (1.0 / OCTAVES) + 0.5
            size = root * root * scales[:, a : a + 1]
            totals[a] = totals[a] + jnp.where(code < 0, -size, size)
    for a in range(layers):
        own_ref[:, a * feature_dev : (a + 1) * feature_dev] = jnp.maximum(totals[a], 0.0).astype(BF16)


def own_features_of(arrived, enc_bias):
    shape = (arrived.shape[1], enc_bias.size)
    return on_chip(
        features_kernel, "own_features", (arrived, enc_bias), jax.ShapeDtypeStruct(shape, BF16)
    )


def decode_kernel(layers, core_ref, features_ref, weight_ref, theirs_ref, mine_ref, held_ref):
    width, feature_dev = weight_ref.shape[1:]
    half = theirs_ref.shape[0]
    core = core_ref[0]
    for b in range(layers):
        total = None
        for a in range(b + 1):
            term = contract(
                features_ref[:, a * feature_dev : (a + 1) * feature_dev],
                weight_ref[pair_number(a, b, layers)],
                1,
                1,
            )
            total = term if total is None else total + term
        held_ref[:, b * width : (b + 1) * width] = total
    for ref, side in ((theirs_ref, 1 - core), (mine_ref, core)):
        ref[...] = held_ref[pl.ds(pl.multiple_of(side * half, half), half), :].astype(ref.dtype)


def decode(core, features, dec_t, layers):
    tokens = features.shape[0]
    columns = layers * dec_t.shape[1]
    return on_chip(
        functools.partial(decode_kernel, layers),
        "decode",
        (core, features, dec_t),
        [jax.ShapeDtypeStruct((tokens // 2, columns), kind) for kind in (BF16, F32)],
        [pltpu.VMEM((tokens, columns), F32)],
    )


def error_kernel(offset_ref, arrived_ref, acts_ref, bias_ref, out_ref):
    chips, rows, _ = arrived_ref.shape
    layers, width, tokens = acts_ref.shape
    row = lax.broadcasted_iota(jnp.int32, (rows, tokens), 0)
    token = lax.broadcasted_iota(jnp.int32, (rows, tokens), 1)
    mine = jnp.where(token == row + offset_ref[0], 1.0, 0.0).astype(BF16)
    total = arrived_ref[0].astype(F32)
    for k in range(1, chips):
        total = total + arrived_ref[k].astype(F32)
    for b in range(layers):
        columns = slice(b * width, (b + 1) * width)
        target = contract(mine, acts_ref[b], 1, 1)
        out_ref[:, columns] = (total[:, columns] + bias_ref[b : b + 1, :] - target).astype(BF16)


def own_error_of(offset, arrived, acts_out_t, dec_bias):
    return on_chip(
        error_kernel,
        "own_error",
        (offset, arrived, acts_out_t, dec_bias),
        jax.ShapeDtypeStruct(arrived.shape[1:], BF16),
    )


def upstream_kernel(layers, error_ref, weight_ref, out_ref):
    tokens = error_ref.shape[0]
    width, feature_dev = weight_ref.shape[1:]
    for a in range(layers):
        total = None
        for b in range(a, layers):
            term = contract(
                error_ref[:, b * width : (b + 1) * width], weight_ref[pair_number(a, b, layers)], 1, 0
            )
            total = term if total is None else total + term
        out_ref[:, a * feature_dev : (a + 1) * feature_dev] = total.astype(BF16)
    wide = error_ref[...].astype(F32)
    squared = jnp.sum(wide * wide)
    coarse = squared.astype(BF16).astype(F32)
    fine = squared - coarse
    lane = lax.broadcasted_iota(jnp.int32, (tokens, LANES), 1)
    extra = jnp.where(lane == 0, coarse, jnp.where(lane == 1, fine, 0.0))
    out_ref[:, layers * feature_dev :] = extra.astype(BF16)


def upstream(error, dec_t, layers):
    shape = (error.shape[0], layers * dec_t.shape[2] + LANES)
    return on_chip(
        functools.partial(upstream_kernel, layers), "upstream", (error, dec_t), jax.ShapeDtypeStruct(shape, BF16)
    )


def encoder_grad_kernel(acts_ref, delta_ref, grad_ref, bias_ref):
    delta = delta_ref[...]
    grad_ref[0] = contract(acts_ref[0], delta, 1, 0)
    bias_ref[pl.ds(pl.program_id(0), 1), :] = jnp.sum(delta.astype(F32), axis=0, keepdims=True)


def encoder_grad(acts_t, delta):
    layers, width, tokens = acts_t.shape
    feature_dev = delta.shape[1] // layers
    return pl.pallas_call(
        encoder_grad_kernel,
        grid=(layers,),
        in_specs=[
            pl.BlockSpec((1, width, tokens), lambda a: (a, 0, 0)),
            pl.BlockSpec((tokens, feature_dev), lambda a: (0, a)),
        ],
        out_specs=[
            pl.BlockSpec((1, width, feature_dev), lambda a: (a, 0, 0)),
            pl.BlockSpec((layers, feature_dev), lambda a: (0, 0)),
        ],
        out_shape=[
            jax.ShapeDtypeStruct((layers, width, feature_dev), F32),
            jax.ShapeDtypeStruct((layers, feature_dev), F32),
        ],
        compiler_params=pltpu.CompilerParams(vmem_limit_bytes=VMEM),
        name="encoder_grad",
    )(acts_t, delta)


def local(acts_in, acts_out, enc_weight, enc_bias, dec_weight, dec_bias):
    layers, tokens, width_dev = acts_in.shape
    feature_dev = enc_weight.shape[2]
    pair_list = [(a, b) for a in range(layers) for b in range(a, layers)]
    slots = lax.axis_size(SLOT)
    chips = lax.axis_size(CHIPS)
    core = lax.axis_index(CORE)
    acts_t = jnp.transpose(acts_in, (0, 2, 1))
    dec_t = jnp.transpose(dec_weight, (0, 2, 1))

    def feats(x, a):
        return x[:, a * feature_dev : (a + 1) * feature_dev]

    def width(x, b):
        return x[:, b * width_dev : (b + 1) * width_dev]

    half = tokens // 2
    portion = half // chips
    core = core.reshape(1)
    offset = core * half + lax.axis_index(CHIPS) * portion
    acts_t, core, offset = lax.optimization_barrier((acts_t, core, offset))

    sent = encode(acts_t, enc_weight)
    arrived = exchange(sent.reshape(slots, tokens // slots, -1), SLOT)
    own_features = own_features_of(arrived, enc_bias)
    features = sent_to_all(own_features, SLOT).reshape(tokens, -1)

    theirs, mine = decode(core, features, dec_t, layers)
    chip_sum = (mine + lax.ppermute(theirs, CORE, [(0, 1), (1, 0)]).astype(F32)).astype(BF16)
    arrived = exchange(chip_sum.reshape(chips, portion, -1), CHIPS)
    own_error = own_error_of(offset, arrived, jnp.transpose(acts_out, (0, 2, 1)), dec_bias)
    half_error = sent_to_all(own_error, CHIPS).reshape(half, -1)
    error = lax.all_gather(half_error, CORE, axis=0, tiled=True)

    sent = upstream(error, dec_t, layers)
    total = exchange(sent.reshape(slots, tokens // slots, -1), SLOT).astype(F32).sum(axis=0)
    mse = (total[0, layers * feature_dev] + total[0, layers * feature_dev + 1]) / (layers * tokens * D)
    own_delta = jnp.where(own_features > 0, total[:, : layers * feature_dev], 0.0).astype(BF16)
    delta = sent_to_all(own_delta, SLOT).reshape(tokens, -1)

    dec_grads = [contract(feats(features, a), width(error, b), 0, 0) for a, b in pair_list]
    enc_grad, bias_grad = encoder_grad(acts_t, delta)
    return (enc_grad, bias_grad, jnp.stack(dec_grads), mse)


def solution(mesh):
    split = Mesh(mesh.devices.reshape(2, 4, 2, 8, 2), (*SLOT, *FEAT))
    in_specs = (
        P(None, None, SLOT),
        P(None, None, SLOT),
        P(None, SLOT, FEAT),
        P(None, FEAT),
        P(None, FEAT, SLOT),
        P(None, SLOT),
    )
    out_specs = (P(None, SLOT, FEAT), P(None, FEAT), P(None, FEAT, SLOT), P())
    return jax.shard_map(local, mesh=split, in_specs=in_specs, out_specs=out_specs, check_vma=False)
```

```python
import functools

import jax
import jax.numpy as jnp
from jax import lax
from jax.experimental import pallas as pl
from jax.experimental.pallas import tpu as pltpu
from jax.sharding import Mesh
from jax.sharding import PartitionSpec as P

D = 2304
SLOT = ("slot_0", "slot_1")
FEAT = ("feat_0", "feat_1", "feat_2")
CHIPS = ("feat_0", "feat_1")
CORE = "feat_2"
LANES = 128
VMEM = 16 * 2**20
OCTAVES = 250.0
ABOVE = 1.0078125
TINY = 1e-30
LEAST = 1e-12
F32 = jnp.float32
BF16 = jnp.bfloat16


def exchange(tiles, axis):
    return lax.all_to_all(tiles, axis, split_axis=0, concat_axis=0, tiled=True)


def sent_to_all(x, axis):
    return exchange(jnp.broadcast_to(x[None], (lax.axis_size(axis), *x.shape)), axis)


def pair_number(a, b, layers):
    return a * layers - a * (a - 1) // 2 + (b - a)


def contract(x, y, x_dim, y_dim):
    return lax.dot_general(x, y, (((x_dim,), (y_dim,)), ((), ())), preferred_element_type=F32)


def encode_kernel(acts_ref, weight_ref, out_ref):
    layers = acts_ref.shape[0]
    tokens = out_ref.shape[0]
    feature_dev = weight_ref.shape[2]
    lane = lax.broadcasted_iota(jnp.int32, (tokens, LANES), 1)
    scales = jnp.zeros((tokens, LANES), F32)
    for a in range(layers):
        preact = contract(acts_ref[a], weight_ref[a], 0, 0)
        size = jnp.abs(preact)
        largest = jnp.maximum(jnp.max(size, axis=1, keepdims=True), TINY)
        scale = (largest * ABOVE).astype(BF16).astype(F32)
        square = jnp.maximum(size * (1.0 / scale), LEAST)
        code = jnp.exp2(square * lax.rsqrt(square) * OCTAVES - OCTAVES / 2)
        out_ref[:, a * feature_dev : (a + 1) * feature_dev] = jnp.where(preact < 0, -code, code).astype(BF16)
        scales = jnp.where(lane == a, scale, scales)
    out_ref[:, layers * feature_dev :] = scales.astype(BF16)


def on_chip(kernel, name, args, out_shape, scratch_shapes=()):
    vmem = pl.BlockSpec(memory_space=pltpu.VMEM)
    smem = pl.BlockSpec(memory_space=pltpu.SMEM)
    return pl.pallas_call(
        kernel,
        in_specs=[smem if arg.dtype == jnp.int32 else vmem for arg in args],
        out_specs=jax.tree.map(lambda _: vmem, out_shape),
        out_shape=out_shape,
        scratch_shapes=scratch_shapes,
        compiler_params=pltpu.CompilerParams(vmem_limit_bytes=VMEM),
        name=name,
    )(*args)


def encode(acts_t, enc_weight):
    layers, _, tokens = acts_t.shape
    shape = (tokens, layers * enc_weight.shape[2] + LANES)
    return on_chip(encode_kernel, "encode", (acts_t, enc_weight), jax.ShapeDtypeStruct(shape, BF16))


def features_kernel(arrived_ref, bias_ref, own_ref):
    slots, rows, _ = arrived_ref.shape
    layers, feature_dev = bias_ref.shape
    totals = [jnp.broadcast_to(bias_ref[a : a + 1, :], (rows, feature_dev)) for a in range(layers)]
    for k in range(slots):
        scales = arrived_ref[k, :, layers * feature_dev :].astype(F32)
        for a in range(layers):
            code = arrived_ref[k, :, a * feature_dev : (a + 1) * feature_dev].astype(F32)
            root = jnp.log2(jnp.abs(code)) * (1.0 / OCTAVES) + 0.5
            size = root * root * scales[:, a : a + 1]
            totals[a] = totals[a] + jnp.where(code < 0, -size, size)
    for a in range(layers):
        own_ref[:, a * feature_dev : (a + 1) * feature_dev] = jnp.maximum(totals[a], 0.0).astype(BF16)


def own_features_of(arrived, enc_bias):
    shape = (arrived.shape[1], enc_bias.size)
    return on_chip(
        features_kernel, "own_features", (arrived, enc_bias), jax.ShapeDtypeStruct(shape, BF16)
    )


def decode_kernel(layers, core_ref, features_ref, weight_ref, theirs_ref, mine_ref, held_ref):
    width, feature_dev = weight_ref.shape[1:]
    half = theirs_ref.shape[0]
    core = core_ref[0]
    for b in range(layers):
        total = None
        for a in range(b + 1):
            term = contract(
                features_ref[:, a * feature_dev : (a + 1) * feature_dev],
                weight_ref[pair_number(a, b, layers)],
                1,
                1,
            )
            total = term if total is None else total + term
        held_ref[:, b * width : (b + 1) * width] = total
    for ref, side in ((theirs_ref, 1 - core), (mine_ref, core)):
        ref[...] = held_ref[pl.ds(pl.multiple_of(side * half, half), half), :].astype(ref.dtype)


def decode(core, features, dec_t, layers):
    tokens = features.shape[0]
    columns = layers * dec_t.shape[1]
    return on_chip(
        functools.partial(decode_kernel, layers),
        "decode",
        (core, features, dec_t),
        [jax.ShapeDtypeStruct((tokens // 2, columns), kind) for kind in (BF16, F32)],
        [pltpu.VMEM((tokens, columns), F32)],
    )


def error_kernel(offset_ref, arrived_ref, acts_ref, bias_ref, out_ref):
    chips, rows, _ = arrived_ref.shape
    layers, width, tokens = acts_ref.shape
    row = lax.broadcasted_iota(jnp.int32, (rows, tokens), 0)
    token = lax.broadcasted_iota(jnp.int32, (rows, tokens), 1)
    mine = jnp.where(token == row + offset_ref[0], 1.0, 0.0).astype(BF16)
    total = arrived_ref[0].astype(F32)
    for k in range(1, chips):
        total = total + arrived_ref[k].astype(F32)
    for b in range(layers):
        columns = slice(b * width, (b + 1) * width)
        target = contract(mine, acts_ref[b], 1, 1)
        out_ref[:, columns] = (total[:, columns] + bias_ref[b : b + 1, :] - target).astype(BF16)


def own_error_of(offset, arrived, acts_out_t, dec_bias):
    return on_chip(
        error_kernel,
        "own_error",
        (offset, arrived, acts_out_t, dec_bias),
        jax.ShapeDtypeStruct(arrived.shape[1:], BF16),
    )


def upstream_kernel(layers, error_ref, weight_ref, out_ref):
    tokens = error_ref.shape[0]
    width, feature_dev = weight_ref.shape[1:]
    for a in range(layers):
        total = None
        for b in range(a, layers):
            term = contract(
                error_ref[:, b * width : (b + 1) * width], weight_ref[pair_number(a, b, layers)], 1, 0
            )
            total = term if total is None else total + term
        out_ref[:, a * feature_dev : (a + 1) * feature_dev] = total.astype(BF16)
    wide = error_ref[...].astype(F32)
    squared = jnp.sum(wide * wide)
    coarse = squared.astype(BF16).astype(F32)
    fine = squared - coarse
    lane = lax.broadcasted_iota(jnp.int32, (tokens, LANES), 1)
    extra = jnp.where(lane == 0, coarse, jnp.where(lane == 1, fine, 0.0))
    out_ref[:, layers * feature_dev :] = extra.astype(BF16)


def upstream(error, dec_t, layers):
    shape = (error.shape[0], layers * dec_t.shape[2] + LANES)
    return on_chip(
        functools.partial(upstream_kernel, layers), "upstream", (error, dec_t), jax.ShapeDtypeStruct(shape, BF16)
    )


def delta_kernel(share, arrived_ref, features_ref, own_ref, mse_ref):
    slots = arrived_ref.shape[0]
    columns = features_ref.shape[1]
    total = arrived_ref[0].astype(F32)
    for k in range(1, slots):
        total = total + arrived_ref[k].astype(F32)
    own_ref[...] = jnp.where(features_ref[...] > 0, total[:, :columns], 0.0).astype(BF16)
    mse_ref[0, 0] = jnp.sum(total[:1, columns:]) * share


def own_delta_of(arrived, own_features, share):
    vmem = pl.BlockSpec(memory_space=pltpu.VMEM)
    return pl.pallas_call(
        functools.partial(delta_kernel, share),
        in_specs=[vmem, vmem],
        out_specs=[vmem, pl.BlockSpec(memory_space=pltpu.SMEM)],
        out_shape=[
            jax.ShapeDtypeStruct(own_features.shape, BF16),
            jax.ShapeDtypeStruct((1, 1), F32),
        ],
        compiler_params=pltpu.CompilerParams(vmem_limit_bytes=VMEM),
        name="own_delta",
    )(arrived, own_features)


def gradients_kernel(
    acts_ref, delta_ref, features_ref, error_ref,
    enc_hbm, bias_ref, dec_hbm, enc_held, dec_held, enc_sems, dec_sems,
):
    layers, width, tokens = acts_ref.shape
    feature_dev = enc_held.shape[2]
    leaving = []

    def send(held, out, sems, k):
        copy = pltpu.make_async_copy(held.at[k], out.at[k], sems.at[k])
        copy.start()
        leaving.append(copy)

    for a in range(layers):
        columns = slice(a * feature_dev, (a + 1) * feature_dev)
        for b in range(a, layers):
            pair = pair_number(a, b, layers)
            dec_held[pair] = contract(error_ref[:, b * width : (b + 1) * width], features_ref[:, columns], 0, 0)
            send(dec_held, dec_hbm, dec_sems, pair)
    ones = jnp.ones((8, tokens), BF16)
    for a in range(layers):
        delta = delta_ref[:, a * feature_dev : (a + 1) * feature_dev]
        enc_held[a] = contract(acts_ref[a], delta, 1, 0)
        send(enc_held, enc_hbm, enc_sems, a)
        bias_ref[a : a + 1, :] = contract(ones, delta, 1, 0)[:1]
    for copy in leaving:
        copy.wait()


def gradients(acts_t, delta, features, error):
    layers, width, tokens = acts_t.shape
    feature_dev = delta.shape[1] // layers
    pairs = layers * (layers + 1) // 2
    vmem = pl.BlockSpec(memory_space=pltpu.VMEM)
    anywhere = pl.BlockSpec(memory_space=pl.ANY)
    enc_shape = (layers, width, feature_dev)
    dec_shape = (pairs, width, feature_dev)
    return pl.pallas_call(
        gradients_kernel,
        in_specs=[vmem] * 4,
        out_specs=[anywhere, vmem, anywhere],
        out_shape=[
            jax.ShapeDtypeStruct(shape, F32) for shape in (enc_shape, (layers, feature_dev), dec_shape)
        ],
        scratch_shapes=[
            pltpu.VMEM(enc_shape, F32),
            pltpu.VMEM(dec_shape, F32),
            pltpu.SemaphoreType.DMA((layers,)),
            pltpu.SemaphoreType.DMA((pairs,)),
        ],
        compiler_params=pltpu.CompilerParams(vmem_limit_bytes=VMEM),
        name="gradients",
    )(acts_t, delta, features, error)


def local(acts_in, acts_out, enc_weight, enc_bias, dec_weight, dec_bias):
    layers, tokens, _ = acts_in.shape
    slots = lax.axis_size(SLOT)
    chips = lax.axis_size(CHIPS)
    core = lax.axis_index(CORE)
    acts_t = jnp.transpose(acts_in, (0, 2, 1))
    dec_t = jnp.transpose(dec_weight, (0, 2, 1))

    half = tokens // 2
    portion = half // chips
    core = core.reshape(1)
    offset = core * half + lax.axis_index(CHIPS) * portion
    sent = encode(acts_t, enc_weight)
    sent, core, offset = lax.optimization_barrier((sent, core, offset))
    arrived = exchange(sent.reshape(slots, tokens // slots, -1), SLOT)
    own_features = own_features_of(arrived, enc_bias)
    features = sent_to_all(own_features, SLOT).reshape(tokens, -1)

    theirs, mine = decode(core, features, dec_t, layers)
    chip_sum = (mine + lax.ppermute(theirs, CORE, [(0, 1), (1, 0)]).astype(F32)).astype(BF16)
    arrived = exchange(chip_sum.reshape(chips, portion, -1), CHIPS)
    own_error = own_error_of(offset, arrived, jnp.transpose(acts_out, (0, 2, 1)), dec_bias)
    half_error = sent_to_all(own_error, CHIPS).reshape(half, -1)
    error = lax.all_gather(half_error, CORE, axis=0, tiled=True)

    sent = upstream(error, dec_t, layers)
    arrived = exchange(sent.reshape(slots, tokens // slots, -1), SLOT)
    own_delta, mse = own_delta_of(arrived, own_features, 1.0 / (layers * tokens * D))
    delta = sent_to_all(own_delta, SLOT).reshape(tokens, -1)
    enc_grad, bias_grad, dec_grad_t = gradients(acts_t, delta, features, error)
    return (enc_grad, bias_grad, jnp.transpose(dec_grad_t, (0, 2, 1)), mse.reshape(()))


def solution(mesh):
    split = Mesh(mesh.devices.reshape(2, 4, 2, 8, 2), (*SLOT, *FEAT))
    in_specs = (
        P(None, None, SLOT),
        P(None, None, SLOT),
        P(None, SLOT, FEAT),
        P(None, FEAT),
        P(None, FEAT, SLOT),
        P(None, SLOT),
    )
    out_specs = (P(None, SLOT, FEAT), P(None, FEAT), P(None, FEAT, SLOT), P())
    return jax.shard_map(local, mesh=split, in_specs=in_specs, out_specs=out_specs, check_vma=False)
```

```python
import functools

import jax
import jax.numpy as jnp
from jax import lax
from jax.experimental import pallas as pl
from jax.experimental.pallas import tpu as pltpu
from jax.sharding import Mesh
from jax.sharding import PartitionSpec as P

D = 2304
SLOT = ("slot_0", "slot_1")
FEAT = ("feat_0", "feat_1", "feat_2")
CHIPS = ("feat_0", "feat_1")
CORE = "feat_2"
LANES = 128
EXTRA = 16
VMEM = 16 * 2**20
OCTAVES = 250.0
ABOVE = 1.0078125
TINY = 1e-30
LEAST = 1e-12
F32 = jnp.float32
BF16 = jnp.bfloat16


def exchange(tiles, axis):
    return lax.all_to_all(tiles, axis, split_axis=0, concat_axis=0, tiled=True)


def sent_to_all(x, axis):
    return exchange(jnp.broadcast_to(x[None], (lax.axis_size(axis), *x.shape)), axis)


def pair_number(a, b, layers):
    return a * layers - a * (a - 1) // 2 + (b - a)


def contract(x, y, x_dim, y_dim):
    return lax.dot_general(x, y, (((x_dim,), (y_dim,)), ((), ())), preferred_element_type=F32)


def store_tiles(out_ref, value, first, slots):
    rows = value.shape[0] // slots
    for k in range(slots):
        for j in range(value.shape[1] // LANES):
            out_ref[k, (first + j) * rows : (first + j + 1) * rows, :] = value[
                k * rows : (k + 1) * rows, j * LANES : (j + 1) * LANES
            ]


def encode_kernel(acts_ref, weight_ref, out_ref):
    layers = acts_ref.shape[0]
    feature_dev = weight_ref.shape[2]
    slots = out_ref.shape[0]
    rows = acts_ref.shape[2] // slots
    tiles = feature_dev // LANES
    scales = []
    for a in range(layers):
        preact = contract(acts_ref[a], weight_ref[a], 0, 0)
        size = jnp.abs(preact)
        largest = jnp.maximum(jnp.max(size, axis=1, keepdims=True), TINY)
        scale = (largest * ABOVE).astype(BF16).astype(F32)
        square = jnp.maximum(size * (1.0 / scale), LEAST)
        code = jnp.exp2(square * lax.rsqrt(square) * OCTAVES - OCTAVES / 2)
        store_tiles(out_ref, jnp.where(preact < 0, -code, code).astype(BF16), a * tiles, slots)
        scales.append(scale)
    lane = lax.broadcasted_iota(jnp.int32, (EXTRA, LANES), 1)
    for k in range(slots):
        extra = jnp.zeros((EXTRA, LANES), F32)
        for part in range(rows // EXTRA):
            at = k * rows + part * EXTRA
            for a in range(layers):
                extra = jnp.where(lane == part * layers + a, scales[a][at : at + EXTRA], extra)
        out_ref[k, layers * tiles * rows :, :] = extra.astype(BF16)


def on_chip(kernel, name, args, out_shape, scratch_shapes=()):
    vmem = pl.BlockSpec(memory_space=pltpu.VMEM)
    smem = pl.BlockSpec(memory_space=pltpu.SMEM)
    return pl.pallas_call(
        kernel,
        in_specs=[smem if arg.dtype == jnp.int32 else vmem for arg in args],
        out_specs=jax.tree.map(lambda _: vmem, out_shape),
        out_shape=out_shape,
        scratch_shapes=scratch_shapes,
        compiler_params=pltpu.CompilerParams(vmem_limit_bytes=VMEM),
        name=name,
    )(*args)


def sent_shape(slots, tokens, columns):
    return jax.ShapeDtypeStruct((slots, tokens // slots * columns // LANES + EXTRA, LANES), BF16)


def encode(acts_t, enc_weight, slots):
    layers, _, tokens = acts_t.shape
    shape = sent_shape(slots, tokens, layers * enc_weight.shape[2])
    return on_chip(encode_kernel, "encode", (acts_t, enc_weight), shape)


def features_kernel(arrived_ref, bias_ref, own_ref):
    slots = arrived_ref.shape[0]
    rows = own_ref.shape[0]
    layers, feature_dev = bias_ref.shape
    tiles = feature_dev // LANES
    scales = []
    for k in range(slots):
        extra = arrived_ref[k, layers * tiles * rows :, :].astype(F32)
        parts = rows // EXTRA
        scales.append(
            [
                jnp.concatenate([extra[:, p * layers + a : p * layers + a + 1] for p in range(parts)], axis=0)
                for a in range(layers)
            ]
        )
    for a in range(layers):
        for j in range(tiles):
            at = (a * tiles + j) * rows
            columns = slice(j * LANES, (j + 1) * LANES)
            total = jnp.broadcast_to(bias_ref[a : a + 1, columns], (rows, LANES))
            for k in range(slots):
                code = arrived_ref[k, at : at + rows, :].astype(F32)
                root = jnp.log2(jnp.abs(code)) * (1.0 / OCTAVES) + 0.5
                size = root * root * scales[k][a]
                total = total + jnp.where(code < 0, -size, size)
            at = (a * tiles + j) * LANES
            own_ref[:, at : at + LANES] = jnp.maximum(total, 0.0).astype(BF16)


def own_features_of(arrived, enc_bias, rows):
    shape = (rows, enc_bias.size)
    return on_chip(
        features_kernel, "own_features", (arrived, enc_bias), jax.ShapeDtypeStruct(shape, BF16)
    )


def decode_kernel(layers, core_ref, features_ref, weight_ref, theirs_ref, mine_ref, held_ref):
    width, feature_dev = weight_ref.shape[1:]
    half = theirs_ref.shape[0]
    core = core_ref[0]
    for b in range(layers):
        total = None
        for a in range(b + 1):
            term = contract(
                features_ref[:, a * feature_dev : (a + 1) * feature_dev],
                weight_ref[pair_number(a, b, layers)],
                1,
                1,
            )
            total = term if total is None else total + term
        held_ref[:, b * width : (b + 1) * width] = total
    for ref, side in ((theirs_ref, 1 - core), (mine_ref, core)):
        ref[...] = held_ref[pl.ds(pl.multiple_of(side * half, half), half), :].astype(ref.dtype)


def decode(core, features, dec_t, layers):
    tokens = features.shape[0]
    columns = layers * dec_t.shape[1]
    return on_chip(
        functools.partial(decode_kernel, layers),
        "decode",
        (core, features, dec_t),
        [jax.ShapeDtypeStruct((tokens // 2, columns), kind) for kind in (BF16, F32)],
        [pltpu.VMEM((tokens, columns), F32)],
    )


def error_kernel(offset_ref, arrived_ref, acts_ref, bias_ref, out_ref):
    chips, rows, _ = arrived_ref.shape
    layers, width, tokens = acts_ref.shape
    row = lax.broadcasted_iota(jnp.int32, (rows, tokens), 0)
    token = lax.broadcasted_iota(jnp.int32, (rows, tokens), 1)
    mine = jnp.where(token == row + offset_ref[0], 1.0, 0.0).astype(BF16)
    total = arrived_ref[0].astype(F32)
    for k in range(1, chips):
        total = total + arrived_ref[k].astype(F32)
    for b in range(layers):
        columns = slice(b * width, (b + 1) * width)
        target = contract(mine, acts_ref[b], 1, 1)
        out_ref[:, columns] = (total[:, columns] + bias_ref[b : b + 1, :] - target).astype(BF16)


def own_error_of(offset, arrived, acts_out_t, dec_bias):
    return on_chip(
        error_kernel,
        "own_error",
        (offset, arrived, acts_out_t, dec_bias),
        jax.ShapeDtypeStruct(arrived.shape[1:], BF16),
    )


def upstream_kernel(layers, core_ref, mine_ref, theirs_ref, weight_ref, out_ref, error_ref):
    width, feature_dev = weight_ref.shape[1:]
    slots = out_ref.shape[0]
    half = mine_ref.shape[0]
    core = core_ref[0]
    for ref, side in ((mine_ref, core), (theirs_ref, 1 - core)):
        error_ref[pl.ds(pl.multiple_of(side * half, half), half), :] = ref[...]
    for a in range(layers):
        total = None
        for b in range(a, layers):
            term = contract(
                error_ref[:, b * width : (b + 1) * width], weight_ref[pair_number(a, b, layers)], 1, 0
            )
            total = term if total is None else total + term
        store_tiles(out_ref, total.astype(BF16), a * feature_dev // LANES, slots)
    wide = error_ref[...].astype(F32)
    squared = jnp.sum(wide * wide)
    coarse = squared.astype(BF16).astype(F32)
    fine = squared - coarse
    lane = lax.broadcasted_iota(jnp.int32, (EXTRA, LANES), 1)
    extra = jnp.where(lane == 0, coarse, jnp.where(lane == 1, fine, 0.0)).astype(BF16)
    for k in range(slots):
        out_ref[k, out_ref.shape[1] - EXTRA :, :] = extra


def upstream(core, mine, theirs, dec_t, layers, slots):
    half, columns = mine.shape
    return on_chip(
        functools.partial(upstream_kernel, layers),
        "upstream",
        (core, mine, theirs, dec_t),
        [
            sent_shape(slots, 2 * half, layers * dec_t.shape[2]),
            jax.ShapeDtypeStruct((2 * half, columns), BF16),
        ],
    )


def delta_kernel(share, arrived_ref, features_ref, own_ref, mse_ref):
    slots = arrived_ref.shape[0]
    rows, columns = features_ref.shape
    total = arrived_ref[0].astype(F32)
    for k in range(1, slots):
        total = total + arrived_ref[k].astype(F32)
    for j in range(columns // LANES):
        at = slice(j * LANES, (j + 1) * LANES)
        delta = jnp.where(features_ref[:, at] > 0, total[j * rows : (j + 1) * rows, :], 0.0)
        own_ref[:, at] = delta.astype(BF16)
    last = columns // LANES * rows
    mse_ref[0, 0] = jnp.sum(total[last : last + 1, :]) * share


def own_delta_of(arrived, own_features, share):
    vmem = pl.BlockSpec(memory_space=pltpu.VMEM)
    return pl.pallas_call(
        functools.partial(delta_kernel, share),
        in_specs=[vmem, vmem],
        out_specs=[vmem, pl.BlockSpec(memory_space=pltpu.SMEM)],
        out_shape=[
            jax.ShapeDtypeStruct(own_features.shape, BF16),
            jax.ShapeDtypeStruct((1, 1), F32),
        ],
        compiler_params=pltpu.CompilerParams(vmem_limit_bytes=VMEM),
        name="own_delta",
    )(arrived, own_features)


def gradients_kernel(
    acts_ref, delta_ref, features_ref, error_ref,
    enc_hbm, bias_ref, dec_hbm, enc_held, dec_held, enc_sems, dec_sems,
):
    layers, width, tokens = acts_ref.shape
    feature_dev = enc_held.shape[2]
    leaving = []

    def send(held, out, sems, k):
        copy = pltpu.make_async_copy(held.at[k], out.at[k], sems.at[k])
        copy.start()
        leaving.append(copy)

    for a in range(layers):
        columns = slice(a * feature_dev, (a + 1) * feature_dev)
        for b in range(a, layers):
            pair = pair_number(a, b, layers)
            dec_held[pair] = contract(error_ref[:, b * width : (b + 1) * width], features_ref[:, columns], 0, 0)
            send(dec_held, dec_hbm, dec_sems, pair)
    ones = jnp.ones((8, tokens), BF16)
    for a in range(layers):
        delta = delta_ref[:, a * feature_dev : (a + 1) * feature_dev]
        enc_held[a] = contract(acts_ref[a], delta, 1, 0)
        send(enc_held, enc_hbm, enc_sems, a)
        bias_ref[a : a + 1, :] = contract(ones, delta, 1, 0)[:1]
    for copy in leaving:
        copy.wait()


def gradients(acts_t, delta, features, error):
    layers, width, tokens = acts_t.shape
    feature_dev = delta.shape[1] // layers
    pairs = layers * (layers + 1) // 2
    vmem = pl.BlockSpec(memory_space=pltpu.VMEM)
    anywhere = pl.BlockSpec(memory_space=pl.ANY)
    enc_shape = (layers, width, feature_dev)
    dec_shape = (pairs, width, feature_dev)
    return pl.pallas_call(
        gradients_kernel,
        in_specs=[vmem] * 4,
        out_specs=[anywhere, vmem, anywhere],
        out_shape=[
            jax.ShapeDtypeStruct(shape, F32) for shape in (enc_shape, (layers, feature_dev), dec_shape)
        ],
        scratch_shapes=[
            pltpu.VMEM(enc_shape, F32),
            pltpu.VMEM(dec_shape, F32),
            pltpu.SemaphoreType.DMA((layers,)),
            pltpu.SemaphoreType.DMA((pairs,)),
        ],
        compiler_params=pltpu.CompilerParams(vmem_limit_bytes=VMEM),
        name="gradients",
    )(acts_t, delta, features, error)


def local(acts_in, acts_out, enc_weight, enc_bias, dec_weight, dec_bias):
    layers, tokens, _ = acts_in.shape
    slots = lax.axis_size(SLOT)
    chips = lax.axis_size(CHIPS)
    core = lax.axis_index(CORE)
    acts_t = jnp.transpose(acts_in, (0, 2, 1))
    dec_t = jnp.transpose(dec_weight, (0, 2, 1))

    half = tokens // 2
    portion = half // chips
    core = core.reshape(1)
    offset = core * half + lax.axis_index(CHIPS) * portion
    sent = encode(acts_t, enc_weight, slots)
    sent, core, offset = lax.optimization_barrier((sent, core, offset))
    own_features = own_features_of(exchange(sent, SLOT), enc_bias, tokens // slots)
    features = sent_to_all(own_features, SLOT).reshape(tokens, -1)

    theirs, mine = decode(core, features, dec_t, layers)
    chip_sum = (mine + lax.ppermute(theirs, CORE, [(0, 1), (1, 0)]).astype(F32)).astype(BF16)
    arrived = exchange(chip_sum.reshape(chips, portion, -1), CHIPS)
    own_error = own_error_of(offset, arrived, jnp.transpose(acts_out, (0, 2, 1)), dec_bias)
    half_error = sent_to_all(own_error, CHIPS).reshape(half, -1)
    other_error = lax.ppermute(half_error, CORE, [(0, 1), (1, 0)])

    sent, error = upstream(core, half_error, other_error, dec_t, layers, slots)
    own_delta, mse = own_delta_of(exchange(sent, SLOT), own_features, 1.0 / (layers * tokens * D))
    delta = sent_to_all(own_delta, SLOT).reshape(tokens, -1)
    enc_grad, bias_grad, dec_grad_t = gradients(acts_t, delta, features, error)
    return (enc_grad, bias_grad, jnp.transpose(dec_grad_t, (0, 2, 1)), mse.reshape(()))


def solution(mesh):
    split = Mesh(mesh.devices.reshape(2, 4, 2, 8, 2), (*SLOT, *FEAT))
    in_specs = (
        P(None, None, SLOT),
        P(None, None, SLOT),
        P(None, SLOT, FEAT),
        P(None, FEAT),
        P(None, FEAT, SLOT),
        P(None, SLOT),
    )
    out_specs = (P(None, SLOT, FEAT), P(None, FEAT), P(None, FEAT, SLOT), P())
    return jax.shard_map(local, mesh=split, in_specs=in_specs, out_specs=out_specs, check_vma=False)
```

```python
import functools

import jax
import jax.numpy as jnp
from jax import lax
from jax.experimental import pallas as pl
from jax.experimental.pallas import tpu as pltpu
from jax.sharding import Mesh
from jax.sharding import PartitionSpec as P

D = 2304
SLOT = ("slot_0", "slot_1")
FEAT = ("feat_0", "feat_1", "feat_2")
CHIPS = ("feat_0", "feat_1")
CORE = "feat_2"
LANES = 128
EXTRA = 16
VMEM = 16 * 2**20
OCTAVES = 250.0
ABOVE = 1.0078125
TINY = 1e-30
LEAST = 1e-12
F32 = jnp.float32
BF16 = jnp.bfloat16


def exchange(tiles, axis):
    return lax.all_to_all(tiles, axis, split_axis=0, concat_axis=0, tiled=True)


def sent_to_all(x, axis):
    return exchange(jnp.broadcast_to(x[None], (lax.axis_size(axis), *x.shape)), axis)


def pair_number(a, b, layers):
    return a * layers - a * (a - 1) // 2 + (b - a)


def contract(x, y, x_dim, y_dim):
    return lax.dot_general(x, y, (((x_dim,), (y_dim,)), ((), ())), preferred_element_type=F32)


def store_tiles(out_ref, value, first, slots):
    rows = value.shape[0] // slots
    for k in range(slots):
        for j in range(value.shape[1] // LANES):
            out_ref[k, (first + j) * rows : (first + j + 1) * rows, :] = value[
                k * rows : (k + 1) * rows, j * LANES : (j + 1) * LANES
            ]


def encode_kernel(acts_ref, weight_ref, out_ref):
    layers = acts_ref.shape[0]
    feature_dev = weight_ref.shape[2]
    slots = out_ref.shape[0]
    rows = acts_ref.shape[2] // slots
    tiles = feature_dev // LANES
    scales = []
    for a in range(layers):
        preact = contract(acts_ref[a], weight_ref[a], 0, 0)
        size = jnp.abs(preact)
        largest = jnp.maximum(jnp.max(size, axis=1, keepdims=True), TINY)
        scale = (largest * ABOVE).astype(BF16).astype(F32)
        square = jnp.maximum(size * (1.0 / scale), LEAST)
        code = jnp.exp2(square * lax.rsqrt(square) * OCTAVES - OCTAVES / 2)
        store_tiles(out_ref, jnp.where(preact < 0, -code, code).astype(BF16), a * tiles, slots)
        scales.append(scale)
    lane = lax.broadcasted_iota(jnp.int32, (EXTRA, LANES), 1)
    for k in range(slots):
        extra = jnp.zeros((EXTRA, LANES), F32)
        for part in range(rows // EXTRA):
            at = k * rows + part * EXTRA
            for a in range(layers):
                extra = jnp.where(lane == part * layers + a, scales[a][at : at + EXTRA], extra)
        out_ref[k, layers * tiles * rows :, :] = extra.astype(BF16)


def on_chip(kernel, name, args, out_shape, flops=None):
    vmem = pl.BlockSpec(memory_space=pltpu.VMEM)
    smem = pl.BlockSpec(memory_space=pltpu.SMEM)
    return pl.pallas_call(
        kernel,
        in_specs=[smem if arg.dtype == jnp.int32 else vmem for arg in args],
        out_specs=jax.tree.map(lambda _: vmem, out_shape),
        out_shape=out_shape,
        compiler_params=pltpu.CompilerParams(vmem_limit_bytes=VMEM),
        cost_estimate=flops and pl.CostEstimate(flops=flops, bytes_accessed=flops // 128, transcendentals=0),
        name=name,
    )(*args)


def sent_shape(slots, tokens, columns):
    return jax.ShapeDtypeStruct((slots, tokens // slots * columns // LANES + EXTRA, LANES), BF16)


def encode(acts_t, enc_weight, slots):
    layers, _, tokens = acts_t.shape
    shape = sent_shape(slots, tokens, layers * enc_weight.shape[2])
    return on_chip(encode_kernel, "encode", (acts_t, enc_weight), shape)


def features_kernel(arrived_ref, bias_ref, own_ref):
    slots = arrived_ref.shape[0]
    rows = own_ref.shape[0]
    layers, feature_dev = bias_ref.shape
    tiles = feature_dev // LANES
    scales = []
    for k in range(slots):
        extra = arrived_ref[k, layers * tiles * rows :, :].astype(F32)
        parts = rows // EXTRA
        scales.append(
            [
                jnp.concatenate([extra[:, p * layers + a : p * layers + a + 1] for p in range(parts)], axis=0)
                for a in range(layers)
            ]
        )
    for a in range(layers):
        for j in range(tiles):
            at = (a * tiles + j) * rows
            columns = slice(j * LANES, (j + 1) * LANES)
            total = jnp.broadcast_to(bias_ref[a : a + 1, columns], (rows, LANES))
            for k in range(slots):
                code = arrived_ref[k, at : at + rows, :].astype(F32)
                root = jnp.log2(jnp.abs(code)) * (1.0 / OCTAVES) + 0.5
                size = root * root * scales[k][a]
                total = total + jnp.where(code < 0, -size, size)
            at = (a * tiles + j) * LANES
            own_ref[:, at : at + LANES] = jnp.maximum(total, 0.0).astype(BF16)


def own_features_of(arrived, enc_bias, rows):
    shape = (rows, enc_bias.size)
    return on_chip(
        features_kernel, "own_features", (arrived, enc_bias), jax.ShapeDtypeStruct(shape, BF16)
    )


def decode_kernel(layers, ours, core_ref, features_ref, weight_ref, out_ref):
    width, feature_dev = weight_ref.shape[1:]
    half = out_ref.shape[0]
    side = core_ref[0] if ours else 1 - core_ref[0]
    rows = pl.ds(pl.multiple_of(side * half, half), half)
    for b in range(layers):
        total = None
        for a in range(b + 1):
            term = contract(
                features_ref[rows, a * feature_dev : (a + 1) * feature_dev],
                weight_ref[pair_number(a, b, layers)],
                1,
                1,
            )
            total = term if total is None else total + term
        out_ref[:, b * width : (b + 1) * width] = total.astype(out_ref.dtype)


def decode(core, features, dec_t, layers, ours):
    half = features.shape[0] // 2
    return on_chip(
        functools.partial(decode_kernel, layers, ours),
        "decode_ours" if ours else "decode_theirs",
        (core, features, dec_t),
        jax.ShapeDtypeStruct((half, layers * dec_t.shape[1]), F32 if ours else BF16),
        2 * half * dec_t.size,
    )


def error_kernel(offset_ref, arrived_ref, acts_ref, bias_ref, out_ref):
    chips, rows, _ = arrived_ref.shape
    layers, width, tokens = acts_ref.shape
    row = lax.broadcasted_iota(jnp.int32, (rows, tokens), 0)
    token = lax.broadcasted_iota(jnp.int32, (rows, tokens), 1)
    mine = jnp.where(token == row + offset_ref[0], 1.0, 0.0).astype(BF16)
    total = arrived_ref[0].astype(F32)
    for k in range(1, chips):
        total = total + arrived_ref[k].astype(F32)
    for b in range(layers):
        columns = slice(b * width, (b + 1) * width)
        target = contract(mine, acts_ref[b], 1, 1)
        out_ref[:, columns] = (total[:, columns] + bias_ref[b : b + 1, :] - target).astype(BF16)


def own_error_of(offset, arrived, acts_out_t, dec_bias):
    return on_chip(
        error_kernel,
        "own_error",
        (offset, arrived, acts_out_t, dec_bias),
        jax.ShapeDtypeStruct(arrived.shape[1:], BF16),
    )


def upstream_rows(layers, error_ref, weight_ref, store):
    width, feature_dev = weight_ref.shape[1:]
    for a in range(layers):
        total = None
        for b in range(a, layers):
            term = contract(
                error_ref[:, b * width : (b + 1) * width], weight_ref[pair_number(a, b, layers)], 1, 0
            )
            total = term if total is None else total + term
        store(total.astype(BF16), a * feature_dev // LANES)


def upstream_ours_kernel(layers, ours_ref, weight_ref, out_ref):
    blocks = out_ref.shape[0]
    upstream_rows(layers, ours_ref, weight_ref, lambda x, first: store_tiles(out_ref, x, first, blocks))


def upstream_ours(ours, dec_t, layers, blocks):
    half = ours.shape[0]
    rows = half // blocks * layers * dec_t.shape[2] // LANES
    return on_chip(
        functools.partial(upstream_ours_kernel, layers),
        "upstream_ours",
        (ours, dec_t),
        jax.ShapeDtypeStruct((blocks, rows, LANES), BF16),
        2 * half * dec_t.size,
    )


def upstream_kernel(layers, core_ref, ours_ref, theirs_ref, sent_ref, weight_ref, out_ref, error_ref):
    blocks, rows, _ = sent_ref.shape
    half = ours_ref.shape[0]
    core = core_ref[0]
    for ref, side in ((ours_ref, core), (theirs_ref, 1 - core)):
        error_ref[pl.ds(pl.multiple_of(side * half, half), half), :] = ref[...]
    for k in range(blocks):
        out_ref[core * blocks + k, :rows, :] = sent_ref[k]
    other = out_ref.at[pl.ds((1 - core) * blocks, blocks)]
    upstream_rows(layers, theirs_ref, weight_ref, lambda x, first: store_tiles(other, x, first, blocks))
    wide = error_ref[...].astype(F32)
    squared = jnp.sum(wide * wide)
    coarse = squared.astype(BF16).astype(F32)
    fine = squared - coarse
    lane = lax.broadcasted_iota(jnp.int32, (EXTRA, LANES), 1)
    extra = jnp.where(lane == 0, coarse, jnp.where(lane == 1, fine, 0.0)).astype(BF16)
    for k in range(2 * blocks):
        out_ref[k, rows:, :] = extra


def upstream(core, ours, theirs, sent_ours, dec_t, layers):
    half, columns = ours.shape
    blocks = sent_ours.shape[0]
    return on_chip(
        functools.partial(upstream_kernel, layers),
        "upstream",
        (core, ours, theirs, sent_ours, dec_t),
        [
            sent_shape(2 * blocks, 2 * half, layers * dec_t.shape[2]),
            jax.ShapeDtypeStruct((2 * half, columns), BF16),
        ],
        2 * half * dec_t.size,
    )


def delta_kernel(share, arrived_ref, features_ref, own_ref, mse_ref):
    slots = arrived_ref.shape[0]
    rows, columns = features_ref.shape
    total = arrived_ref[0].astype(F32)
    for k in range(1, slots):
        total = total + arrived_ref[k].astype(F32)
    for j in range(columns // LANES):
        at = slice(j * LANES, (j + 1) * LANES)
        delta = jnp.where(features_ref[:, at] > 0, total[j * rows : (j + 1) * rows, :], 0.0)
        own_ref[:, at] = delta.astype(BF16)
    last = columns // LANES * rows
    mse_ref[0, 0] = jnp.sum(total[last : last + 1, :]) * share


def own_delta_of(arrived, own_features, share):
    vmem = pl.BlockSpec(memory_space=pltpu.VMEM)
    return pl.pallas_call(
        functools.partial(delta_kernel, share),
        in_specs=[vmem, vmem],
        out_specs=[vmem, pl.BlockSpec(memory_space=pltpu.SMEM)],
        out_shape=[
            jax.ShapeDtypeStruct(own_features.shape, BF16),
            jax.ShapeDtypeStruct((1, 1), F32),
        ],
        compiler_params=pltpu.CompilerParams(vmem_limit_bytes=VMEM),
        name="own_delta",
    )(arrived, own_features)


def gradients_kernel(
    acts_ref, delta_ref, features_ref, error_ref,
    enc_hbm, bias_ref, dec_hbm, enc_held, dec_held, enc_sems, dec_sems,
):
    layers, width, tokens = acts_ref.shape
    feature_dev = enc_held.shape[2]
    leaving = []

    def send(held, out, sems, k):
        copy = pltpu.make_async_copy(held.at[k], out.at[k], sems.at[k])
        copy.start()
        leaving.append(copy)

    for a in range(layers):
        columns = slice(a * feature_dev, (a + 1) * feature_dev)
        for b in range(a, layers):
            pair = pair_number(a, b, layers)
            dec_held[pair] = contract(error_ref[:, b * width : (b + 1) * width], features_ref[:, columns], 0, 0)
            send(dec_held, dec_hbm, dec_sems, pair)
    ones = jnp.ones((8, tokens), BF16)
    for a in range(layers):
        delta = delta_ref[:, a * feature_dev : (a + 1) * feature_dev]
        enc_held[a] = contract(acts_ref[a], delta, 1, 0)
        send(enc_held, enc_hbm, enc_sems, a)
        bias_ref[a : a + 1, :] = contract(ones, delta, 1, 0)[:1]
    for copy in leaving:
        copy.wait()


def gradients(acts_t, delta, features, error):
    layers, width, tokens = acts_t.shape
    feature_dev = delta.shape[1] // layers
    pairs = layers * (layers + 1) // 2
    vmem = pl.BlockSpec(memory_space=pltpu.VMEM)
    anywhere = pl.BlockSpec(memory_space=pl.ANY)
    enc_shape = (layers, width, feature_dev)
    dec_shape = (pairs, width, feature_dev)
    return pl.pallas_call(
        gradients_kernel,
        in_specs=[vmem] * 4,
        out_specs=[anywhere, vmem, anywhere],
        out_shape=[
            jax.ShapeDtypeStruct(shape, F32) for shape in (enc_shape, (layers, feature_dev), dec_shape)
        ],
        scratch_shapes=[
            pltpu.VMEM(enc_shape, F32),
            pltpu.VMEM(dec_shape, F32),
            pltpu.SemaphoreType.DMA((layers,)),
            pltpu.SemaphoreType.DMA((pairs,)),
        ],
        compiler_params=pltpu.CompilerParams(vmem_limit_bytes=VMEM),
        name="gradients",
    )(acts_t, delta, features, error)


def local(acts_in, acts_out, enc_weight, enc_bias, dec_weight, dec_bias):
    layers, tokens, _ = acts_in.shape
    slots = lax.axis_size(SLOT)
    chips = lax.axis_size(CHIPS)
    core = lax.axis_index(CORE)
    acts_t = jnp.transpose(acts_in, (0, 2, 1))
    dec_t = jnp.transpose(dec_weight, (0, 2, 1))

    half = tokens // 2
    portion = half // chips
    core = core.reshape(1)
    offset = core * half + lax.axis_index(CHIPS) * portion
    sent = encode(acts_t, enc_weight, slots)
    sent, core, offset = lax.optimization_barrier((sent, core, offset))
    own_features = own_features_of(exchange(sent, SLOT), enc_bias, tokens // slots)
    features = sent_to_all(own_features, SLOT).reshape(tokens, -1)

    swap = [(0, 1), (1, 0)]
    from_core = lax.ppermute(decode(core, features, dec_t, layers, False), CORE, swap)
    chip_sum = (decode(core, features, dec_t, layers, True) + from_core.astype(F32)).astype(BF16)
    arrived = exchange(chip_sum.reshape(chips, portion, -1), CHIPS)
    own_error = own_error_of(offset, arrived, jnp.transpose(acts_out, (0, 2, 1)), dec_bias)
    half_error = sent_to_all(own_error, CHIPS).reshape(half, -1)
    other_error = lax.ppermute(half_error, CORE, swap)
    sent_ours = upstream_ours(half_error, dec_t, layers, slots // 2)
    sent, error = upstream(core, half_error, other_error, sent_ours, dec_t, layers)
    own_delta, mse = own_delta_of(exchange(sent, SLOT), own_features, 1.0 / (layers * tokens * D))
    delta = sent_to_all(own_delta, SLOT).reshape(tokens, -1)
    enc_grad, bias_grad, dec_grad_t = gradients(acts_t, delta, features, error)
    return (enc_grad, bias_grad, jnp.transpose(dec_grad_t, (0, 2, 1)), mse.reshape(()))


def solution(mesh):
    split = Mesh(mesh.devices.reshape(2, 4, 2, 8, 2), (*SLOT, *FEAT))
    in_specs = (
        P(None, None, SLOT),
        P(None, None, SLOT),
        P(None, SLOT, FEAT),
        P(None, FEAT),
        P(None, FEAT, SLOT),
        P(None, SLOT),
    )
    out_specs = (P(None, SLOT, FEAT), P(None, FEAT), P(None, FEAT, SLOT), P())
    return jax.shard_map(local, mesh=split, in_specs=in_specs, out_specs=out_specs, check_vma=False)
```

```python
import functools

import jax
import jax.numpy as jnp
from jax import lax
from jax.experimental import pallas as pl
from jax.experimental.pallas import tpu as pltpu
from jax.sharding import Mesh
from jax.sharding import PartitionSpec as P

D = 2304
SLOT = ("slot_0", "slot_1")
FEAT = ("feat_0", "feat_1", "feat_2")
CHIPS = ("feat_0", "feat_1")
CORE = "feat_2"
LANES = 128
EXTRA = 16
VMEM = 16 * 2**20
ALONE = 56 * 2**20
OCTAVES = 250.0
ABOVE = 1.0078125
TINY = 1e-30
LEAST = 1e-12
F32 = jnp.float32
BF16 = jnp.bfloat16


def exchange(tiles, axis):
    return lax.all_to_all(tiles, axis, split_axis=0, concat_axis=0, tiled=True)


def sent_to_all(x, axis):
    return exchange(jnp.broadcast_to(x[None], (lax.axis_size(axis), *x.shape)), axis)


def pair_number(a, b, layers):
    return a * layers - a * (a - 1) // 2 + (b - a)


def contract(x, y, x_dim, y_dim):
    return lax.dot_general(x, y, (((x_dim,), (y_dim,)), ((), ())), preferred_element_type=F32)


def store_tiles(out_ref, value, first, slots):
    rows = value.shape[0] // slots
    for k in range(slots):
        for j in range(value.shape[1] // LANES):
            out_ref[k, (first + j) * rows : (first + j + 1) * rows, :] = value[
                k * rows : (k + 1) * rows, j * LANES : (j + 1) * LANES
            ]


def encode_kernel(acts_hbm, weight_hbm, out_ref, acts_ref, weight_ref, acts_sems, weight_sems):
    layers = acts_ref.shape[0]
    arriving = []
    for a in range(layers):
        for source, held, sems in ((weight_hbm, weight_ref, weight_sems), (acts_hbm, acts_ref, acts_sems)):
            copy = pltpu.make_async_copy(source.at[a], held.at[a], sems.at[a])
            copy.start()
            arriving.append(copy)
    feature_dev = weight_ref.shape[2]
    slots = out_ref.shape[0]
    rows = acts_ref.shape[2] // slots
    tiles = feature_dev // LANES
    scales = []
    for a in range(layers):
        arriving[2 * a].wait()
        arriving[2 * a + 1].wait()
        preact = contract(acts_ref[a], weight_ref[a], 0, 0)
        size = jnp.abs(preact)
        largest = jnp.maximum(jnp.max(size, axis=1, keepdims=True), TINY)
        scale = (largest * ABOVE).astype(BF16).astype(F32)
        square = jnp.maximum(size * (1.0 / scale), LEAST)
        code = jnp.exp2(square * lax.rsqrt(square) * OCTAVES - OCTAVES / 2)
        store_tiles(out_ref, jnp.where(preact < 0, -code, code).astype(BF16), a * tiles, slots)
        scales.append(scale)
    lane = lax.broadcasted_iota(jnp.int32, (EXTRA, LANES), 1)
    for k in range(slots):
        extra = jnp.zeros((EXTRA, LANES), F32)
        for part in range(rows // EXTRA):
            at = k * rows + part * EXTRA
            for a in range(layers):
                extra = jnp.where(lane == part * layers + a, scales[a][at : at + EXTRA], extra)
        out_ref[k, layers * tiles * rows :, :] = extra.astype(BF16)


def on_chip(kernel, name, args, out_shape, flops=None):
    vmem = pl.BlockSpec(memory_space=pltpu.VMEM)
    smem = pl.BlockSpec(memory_space=pltpu.SMEM)
    return pl.pallas_call(
        kernel,
        in_specs=[smem if arg.dtype == jnp.int32 else vmem for arg in args],
        out_specs=jax.tree.map(lambda _: vmem, out_shape),
        out_shape=out_shape,
        compiler_params=pltpu.CompilerParams(vmem_limit_bytes=VMEM),
        cost_estimate=flops and pl.CostEstimate(flops=flops, bytes_accessed=flops // 128, transcendentals=0),
        name=name,
    )(*args)


def sent_shape(slots, tokens, columns):
    return jax.ShapeDtypeStruct((slots, tokens // slots * columns // LANES + EXTRA, LANES), BF16)


def encode(acts_t, enc_weight, slots):
    layers, _, tokens = acts_t.shape
    shape = sent_shape(slots, tokens, layers * enc_weight.shape[2])
    anywhere = pl.BlockSpec(memory_space=pl.ANY)
    return pl.pallas_call(
        encode_kernel,
        in_specs=[anywhere, anywhere],
        out_specs=pl.BlockSpec(memory_space=pltpu.VMEM),
        out_shape=pltpu.VMEM(shape.shape, shape.dtype),
        scratch_shapes=[
            pltpu.VMEM(acts_t.shape, BF16),
            pltpu.VMEM(enc_weight.shape, BF16),
            pltpu.SemaphoreType.DMA((layers,)),
            pltpu.SemaphoreType.DMA((layers,)),
        ],
        compiler_params=pltpu.CompilerParams(vmem_limit_bytes=ALONE),
        name="encode",
    )(acts_t, enc_weight)


def features_kernel(arrived_ref, bias_ref, own_ref):
    slots = arrived_ref.shape[0]
    rows = own_ref.shape[0]
    layers, feature_dev = bias_ref.shape
    tiles = feature_dev // LANES
    scales = []
    for k in range(slots):
        extra = arrived_ref[k, layers * tiles * rows :, :].astype(F32)
        parts = rows // EXTRA
        scales.append(
            [
                jnp.concatenate([extra[:, p * layers + a : p * layers + a + 1] for p in range(parts)], axis=0)
                for a in range(layers)
            ]
        )
    for a in range(layers):
        for j in range(tiles):
            at = (a * tiles + j) * rows
            columns = slice(j * LANES, (j + 1) * LANES)
            total = jnp.broadcast_to(bias_ref[a : a + 1, columns], (rows, LANES))
            for k in range(slots):
                code = arrived_ref[k, at : at + rows, :].astype(F32)
                root = jnp.log2(jnp.abs(code)) * (1.0 / OCTAVES) + 0.5
                size = root * root * scales[k][a]
                total = total + jnp.where(code < 0, -size, size)
            at = (a * tiles + j) * LANES
            own_ref[:, at : at + LANES] = jnp.maximum(total, 0.0).astype(BF16)


def own_features_of(arrived, enc_bias, rows):
    shape = (rows, enc_bias.size)
    return on_chip(
        features_kernel, "own_features", (arrived, enc_bias), jax.ShapeDtypeStruct(shape, BF16)
    )


def decode_kernel(layers, ours, core_ref, features_ref, weight_ref, out_ref):
    width, feature_dev = weight_ref.shape[1:]
    half = out_ref.shape[0]
    side = core_ref[0] if ours else 1 - core_ref[0]
    rows = pl.ds(pl.multiple_of(side * half, half), half)
    for b in range(layers):
        total = None
        for a in range(b + 1):
            term = contract(
                features_ref[rows, a * feature_dev : (a + 1) * feature_dev],
                weight_ref[pair_number(a, b, layers)],
                1,
                1,
            )
            total = term if total is None else total + term
        out_ref[:, b * width : (b + 1) * width] = total.astype(out_ref.dtype)


def decode(core, features, dec_t, layers, ours):
    half = features.shape[0] // 2
    return on_chip(
        functools.partial(decode_kernel, layers, ours),
        "decode_ours" if ours else "decode_theirs",
        (core, features, dec_t),
        jax.ShapeDtypeStruct((half, layers * dec_t.shape[1]), F32 if ours else BF16),
        2 * half * dec_t.size,
    )


def error_kernel(offset_ref, arrived_ref, acts_ref, bias_ref, out_ref):
    chips, rows, _ = arrived_ref.shape
    layers, width, tokens = acts_ref.shape
    row = lax.broadcasted_iota(jnp.int32, (rows, tokens), 0)
    token = lax.broadcasted_iota(jnp.int32, (rows, tokens), 1)
    mine = jnp.where(token == row + offset_ref[0], 1.0, 0.0).astype(BF16)
    total = arrived_ref[0].astype(F32)
    for k in range(1, chips):
        total = total + arrived_ref[k].astype(F32)
    for b in range(layers):
        columns = slice(b * width, (b + 1) * width)
        target = contract(mine, acts_ref[b], 1, 1)
        out_ref[:, columns] = (total[:, columns] + bias_ref[b : b + 1, :] - target).astype(BF16)


def own_error_of(offset, arrived, acts_out_t, dec_bias):
    return on_chip(
        error_kernel,
        "own_error",
        (offset, arrived, acts_out_t, dec_bias),
        jax.ShapeDtypeStruct(arrived.shape[1:], BF16),
    )


def upstream_rows(layers, error_ref, weight_ref, store):
    width, feature_dev = weight_ref.shape[1:]
    for a in range(layers):
        total = None
        for b in range(a, layers):
            term = contract(
                error_ref[:, b * width : (b + 1) * width], weight_ref[pair_number(a, b, layers)], 1, 0
            )
            total = term if total is None else total + term
        store(total.astype(BF16), a * feature_dev // LANES)


def upstream_ours_kernel(layers, ours_ref, weight_ref, out_ref):
    blocks = out_ref.shape[0]
    upstream_rows(layers, ours_ref, weight_ref, lambda x, first: store_tiles(out_ref, x, first, blocks))


def upstream_ours(ours, dec_t, layers, blocks):
    half = ours.shape[0]
    rows = half // blocks * layers * dec_t.shape[2] // LANES
    return on_chip(
        functools.partial(upstream_ours_kernel, layers),
        "upstream_ours",
        (ours, dec_t),
        jax.ShapeDtypeStruct((blocks, rows, LANES), BF16),
        2 * half * dec_t.size,
    )


def upstream_kernel(layers, core_ref, ours_ref, theirs_ref, sent_ref, weight_ref, out_ref, error_ref):
    blocks, rows, _ = sent_ref.shape
    half = ours_ref.shape[0]
    core = core_ref[0]
    for ref, side in ((ours_ref, core), (theirs_ref, 1 - core)):
        error_ref[pl.ds(pl.multiple_of(side * half, half), half), :] = ref[...]
    for k in range(blocks):
        out_ref[core * blocks + k, :rows, :] = sent_ref[k]
    other = out_ref.at[pl.ds((1 - core) * blocks, blocks)]
    upstream_rows(layers, theirs_ref, weight_ref, lambda x, first: store_tiles(other, x, first, blocks))
    wide = error_ref[...].astype(F32)
    squared = jnp.sum(wide * wide)
    coarse = squared.astype(BF16).astype(F32)
    fine = squared - coarse
    lane = lax.broadcasted_iota(jnp.int32, (EXTRA, LANES), 1)
    extra = jnp.where(lane == 0, coarse, jnp.where(lane == 1, fine, 0.0)).astype(BF16)
    for k in range(2 * blocks):
        out_ref[k, rows:, :] = extra


def upstream(core, ours, theirs, sent_ours, dec_t, layers):
    half, columns = ours.shape
    blocks = sent_ours.shape[0]
    return on_chip(
        functools.partial(upstream_kernel, layers),
        "upstream",
        (core, ours, theirs, sent_ours, dec_t),
        [
            sent_shape(2 * blocks, 2 * half, layers * dec_t.shape[2]),
            jax.ShapeDtypeStruct((2 * half, columns), BF16),
        ],
        2 * half * dec_t.size,
    )


def delta_kernel(arrived_ref, features_ref, own_ref, extra_ref):
    slots = arrived_ref.shape[0]
    rows, columns = features_ref.shape
    total = arrived_ref[0].astype(F32)
    for k in range(1, slots):
        total = total + arrived_ref[k].astype(F32)
    for j in range(columns // LANES):
        at = slice(j * LANES, (j + 1) * LANES)
        delta = jnp.where(features_ref[:, at] > 0, total[j * rows : (j + 1) * rows, :], 0.0)
        own_ref[:, at] = delta.astype(BF16)
    last = columns // LANES * rows
    extra_ref[...] = total[last : last + EXTRA, :]


def own_delta_of(arrived, own_features):
    return on_chip(
        delta_kernel,
        "own_delta",
        (arrived, own_features),
        [pltpu.VMEM(own_features.shape, BF16), pltpu.VMEM((EXTRA, LANES), F32)],
    )


def gradients_kernel(
    share, acts_ref, delta_ref, features_ref, error_ref, extra_ref,
    enc_hbm, bias_hbm, dec_hbm, mse_hbm,
    enc_held, bias_held, dec_held, mse_held, enc_sems, dec_sems, small_sems,
):
    layers, width, tokens = acts_ref.shape
    feature_dev = enc_held.shape[2]
    leaving = []

    def send(held, out, sem):
        copy = pltpu.make_async_copy(held, out, sem)
        copy.start()
        leaving.append(copy)

    def layer(a):
        return slice(a * feature_dev, (a + 1) * feature_dev)

    for a in range(layers):
        for b in range(a, layers):
            pair = pair_number(a, b, layers)
            dec_held[pair] = contract(
                error_ref[:, b * width : (b + 1) * width], features_ref[:, layer(a)], 0, 0
            )
            send(dec_held.at[pair], dec_hbm.at[pair], dec_sems.at[pair])
    mse_held[...] = jnp.sum(extra_ref[:1, :], axis=1, keepdims=True) * share
    send(mse_held, mse_hbm, small_sems.at[0])
    ones = jnp.ones((8, tokens), BF16)
    for a in range(layers):
        bias_held[a : a + 1, :] = contract(ones, delta_ref[:, layer(a)], 1, 0)[:1]
    send(bias_held, bias_hbm, small_sems.at[1])
    for a in range(layers):
        enc_held[a] = contract(acts_ref[a], delta_ref[:, layer(a)], 1, 0)
        send(enc_held.at[a], enc_hbm.at[a], enc_sems.at[a])
    for copy in leaving:
        copy.wait()


def gradients(acts_t, delta, features, error, extra, share):
    layers, width, _ = acts_t.shape
    feature_dev = delta.shape[1] // layers
    pairs = layers * (layers + 1) // 2
    vmem = pl.BlockSpec(memory_space=pltpu.VMEM)
    anywhere = pl.BlockSpec(memory_space=pl.ANY)
    shapes = (
        (layers, width, feature_dev),
        (layers, feature_dev),
        (pairs, width, feature_dev),
        (1, 1),
    )
    return pl.pallas_call(
        functools.partial(gradients_kernel, share),
        in_specs=[vmem] * 5,
        out_specs=[anywhere] * 4,
        out_shape=[jax.ShapeDtypeStruct(shape, F32) for shape in shapes],
        scratch_shapes=[pltpu.VMEM(shape, F32) for shape in shapes]
        + [pltpu.SemaphoreType.DMA((count,)) for count in (layers, pairs, 2)],
        compiler_params=pltpu.CompilerParams(vmem_limit_bytes=VMEM),
        name="gradients",
    )(acts_t, delta, features, error, extra)


def local(acts_in, acts_out, enc_weight, enc_bias, dec_weight, dec_bias):
    layers, tokens, _ = acts_in.shape
    slots = lax.axis_size(SLOT)
    chips = lax.axis_size(CHIPS)
    core = lax.axis_index(CORE)
    acts_t = jnp.transpose(acts_in, (0, 2, 1))
    dec_t = jnp.transpose(dec_weight, (0, 2, 1))

    half = tokens // 2
    portion = half // chips
    core = core.reshape(1)
    offset = core * half + lax.axis_index(CHIPS) * portion
    sent = encode(acts_t, enc_weight, slots)
    sent, core, offset = lax.optimization_barrier((sent, core, offset))
    own_features = own_features_of(exchange(sent, SLOT), enc_bias, tokens // slots)
    features = sent_to_all(own_features, SLOT).reshape(tokens, -1)

    swap = [(0, 1), (1, 0)]
    from_core = lax.ppermute(decode(core, features, dec_t, layers, False), CORE, swap)
    chip_sum = (decode(core, features, dec_t, layers, True) + from_core.astype(F32)).astype(BF16)
    arrived = exchange(chip_sum.reshape(chips, portion, -1), CHIPS)
    own_error = own_error_of(offset, arrived, jnp.transpose(acts_out, (0, 2, 1)), dec_bias)
    half_error = sent_to_all(own_error, CHIPS).reshape(half, -1)
    other_error = lax.ppermute(half_error, CORE, swap)
    sent_ours = upstream_ours(half_error, dec_t, layers, slots // 2)
    sent, error = upstream(core, half_error, other_error, sent_ours, dec_t, layers)
    own_delta, extra = own_delta_of(exchange(sent, SLOT), own_features)
    delta = sent_to_all(own_delta, SLOT).reshape(tokens, -1)
    share = 1.0 / (layers * tokens * D)
    enc_grad, bias_grad, dec_grad_t, mse = gradients(acts_t, delta, features, error, extra, share)
    return (enc_grad, bias_grad, jnp.transpose(dec_grad_t, (0, 2, 1)), mse.reshape(()))


def solution(mesh):
    split = Mesh(mesh.devices.reshape(2, 4, 2, 8, 2), (*SLOT, *FEAT))
    in_specs = (
        P(None, None, SLOT),
        P(None, None, SLOT),
        P(None, SLOT, FEAT),
        P(None, FEAT),
        P(None, FEAT, SLOT),
        P(None, SLOT),
    )
    out_specs = (P(None, SLOT, FEAT), P(None, FEAT), P(None, FEAT, SLOT), P())
    return jax.shard_map(local, mesh=split, in_specs=in_specs, out_specs=out_specs, check_vma=False)
```

```python
import functools

import jax
import jax.numpy as jnp
from jax import lax
from jax.experimental import pallas as pl
from jax.experimental.pallas import tpu as pltpu
from jax.sharding import Mesh
from jax.sharding import PartitionSpec as P

D = 2304
SLOT = ("slot_0", "slot_1")
FEAT = ("feat_0", "feat_1", "feat_2")
CHIPS = ("feat_0", "feat_1")
CORE = "feat_2"
LANES = 128
EXTRA = 16
EARLY = 1
VMEM = 16 * 2**20
ALONE = 56 * 2**20
OCTAVES = 250.0
ABOVE = 1.0078125
TINY = 1e-30
LEAST = 1e-12
F32 = jnp.float32
BF16 = jnp.bfloat16


def exchange(tiles, axis):
    return lax.all_to_all(tiles, axis, split_axis=0, concat_axis=0, tiled=True)


def sent_to_all(x, axis):
    return exchange(jnp.broadcast_to(x[None], (lax.axis_size(axis), *x.shape)), axis)


def pair_number(a, b, layers):
    return a * layers - a * (a - 1) // 2 + (b - a)


def contract(x, y, x_dim, y_dim):
    return lax.dot_general(x, y, (((x_dim,), (y_dim,)), ((), ())), preferred_element_type=F32)


def store_tiles(out_ref, value, first, slots):
    rows = value.shape[0] // slots
    for k in range(slots):
        for j in range(value.shape[1] // LANES):
            out_ref[k, (first + j) * rows : (first + j + 1) * rows, :] = value[
                k * rows : (k + 1) * rows, j * LANES : (j + 1) * LANES
            ]


def encode_kernel(acts_hbm, weight_hbm, out_ref, acts_ref, weight_ref, acts_sems, weight_sems):
    layers = acts_ref.shape[0]
    arriving = []
    for a in range(layers):
        for source, held, sems in ((weight_hbm, weight_ref, weight_sems), (acts_hbm, acts_ref, acts_sems)):
            copy = pltpu.make_async_copy(source.at[a], held.at[a], sems.at[a])
            copy.start()
            arriving.append(copy)
    feature_dev = weight_ref.shape[2]
    slots = out_ref.shape[0]
    rows = acts_ref.shape[2] // slots
    tiles = feature_dev // LANES
    scales = []
    for a in range(layers):
        arriving[2 * a].wait()
        arriving[2 * a + 1].wait()
        preact = contract(acts_ref[a], weight_ref[a], 0, 0)
        size = jnp.abs(preact)
        largest = jnp.maximum(jnp.max(size, axis=1, keepdims=True), TINY)
        scale = (largest * ABOVE).astype(BF16).astype(F32)
        square = jnp.maximum(size * (1.0 / scale), LEAST)
        code = jnp.exp2(square * lax.rsqrt(square) * OCTAVES - OCTAVES / 2)
        store_tiles(out_ref, jnp.where(preact < 0, -code, code).astype(BF16), a * tiles, slots)
        scales.append(scale)
    lane = lax.broadcasted_iota(jnp.int32, (EXTRA, LANES), 1)
    for k in range(slots):
        extra = jnp.zeros((EXTRA, LANES), F32)
        for part in range(rows // EXTRA):
            at = k * rows + part * EXTRA
            for a in range(layers):
                extra = jnp.where(lane == part * layers + a, scales[a][at : at + EXTRA], extra)
        out_ref[k, layers * tiles * rows :, :] = extra.astype(BF16)


def on_chip(kernel, name, args, out_shape, flops=None):
    vmem = pl.BlockSpec(memory_space=pltpu.VMEM)
    smem = pl.BlockSpec(memory_space=pltpu.SMEM)
    return pl.pallas_call(
        kernel,
        in_specs=[smem if arg.dtype == jnp.int32 else vmem for arg in args],
        out_specs=jax.tree.map(lambda _: vmem, out_shape),
        out_shape=out_shape,
        compiler_params=pltpu.CompilerParams(vmem_limit_bytes=VMEM),
        cost_estimate=flops and pl.CostEstimate(flops=flops, bytes_accessed=flops // 128, transcendentals=0),
        name=name,
    )(*args)


def sent_shape(slots, tokens, columns):
    return jax.ShapeDtypeStruct((slots, tokens // slots * columns // LANES + EXTRA, LANES), BF16)


def encode(acts_t, enc_weight, slots):
    layers, _, tokens = acts_t.shape
    shape = sent_shape(slots, tokens, layers * enc_weight.shape[2])
    anywhere = pl.BlockSpec(memory_space=pl.ANY)
    return pl.pallas_call(
        encode_kernel,
        in_specs=[anywhere, anywhere],
        out_specs=pl.BlockSpec(memory_space=pltpu.VMEM),
        out_shape=pltpu.VMEM(shape.shape, shape.dtype),
        scratch_shapes=[
            pltpu.VMEM(acts_t.shape, BF16),
            pltpu.VMEM(enc_weight.shape, BF16),
            pltpu.SemaphoreType.DMA((layers,)),
            pltpu.SemaphoreType.DMA((layers,)),
        ],
        compiler_params=pltpu.CompilerParams(vmem_limit_bytes=ALONE),
        name="encode",
    )(acts_t, enc_weight)


def features_kernel(arrived_ref, bias_ref, own_ref):
    slots = arrived_ref.shape[0]
    rows = own_ref.shape[0]
    layers, feature_dev = bias_ref.shape
    tiles = feature_dev // LANES
    scales = []
    for k in range(slots):
        extra = arrived_ref[k, layers * tiles * rows :, :].astype(F32)
        parts = rows // EXTRA
        scales.append(
            [
                jnp.concatenate([extra[:, p * layers + a : p * layers + a + 1] for p in range(parts)], axis=0)
                for a in range(layers)
            ]
        )
    for a in range(layers):
        for j in range(tiles):
            at = (a * tiles + j) * rows
            columns = slice(j * LANES, (j + 1) * LANES)
            total = jnp.broadcast_to(bias_ref[a : a + 1, columns], (rows, LANES))
            for k in range(slots):
                code = arrived_ref[k, at : at + rows, :].astype(F32)
                root = jnp.log2(jnp.abs(code)) * (1.0 / OCTAVES) + 0.5
                size = root * root * scales[k][a]
                total = total + jnp.where(code < 0, -size, size)
            at = (a * tiles + j) * LANES
            own_ref[:, at : at + LANES] = jnp.maximum(total, 0.0).astype(BF16)


def own_features_of(arrived, enc_bias, rows):
    shape = (rows, enc_bias.size)
    return on_chip(
        features_kernel, "own_features", (arrived, enc_bias), jax.ShapeDtypeStruct(shape, BF16)
    )


def decode_kernel(layers, ours, core_ref, features_ref, weight_ref, out_ref):
    width, feature_dev = weight_ref.shape[1:]
    half = out_ref.shape[0]
    side = core_ref[0] if ours else 1 - core_ref[0]
    rows = pl.ds(pl.multiple_of(side * half, half), half)
    for b in range(layers):
        total = None
        for a in range(b + 1):
            term = contract(
                features_ref[rows, a * feature_dev : (a + 1) * feature_dev],
                weight_ref[pair_number(a, b, layers)],
                1,
                1,
            )
            total = term if total is None else total + term
        out_ref[:, b * width : (b + 1) * width] = total.astype(out_ref.dtype)


def decode(core, features, dec_t, layers, ours):
    half = features.shape[0] // 2
    return on_chip(
        functools.partial(decode_kernel, layers, ours),
        "decode_ours" if ours else "decode_theirs",
        (core, features, dec_t),
        jax.ShapeDtypeStruct((half, layers * dec_t.shape[1]), F32 if ours else BF16),
        2 * half * dec_t.size,
    )


def error_kernel(offset_ref, arrived_ref, acts_ref, bias_ref, out_ref):
    chips, rows, _ = arrived_ref.shape
    layers, width, tokens = acts_ref.shape
    row = lax.broadcasted_iota(jnp.int32, (rows, tokens), 0)
    token = lax.broadcasted_iota(jnp.int32, (rows, tokens), 1)
    mine = jnp.where(token == row + offset_ref[0], 1.0, 0.0).astype(BF16)
    total = arrived_ref[0].astype(F32)
    for k in range(1, chips):
        total = total + arrived_ref[k].astype(F32)
    for b in range(layers):
        columns = slice(b * width, (b + 1) * width)
        target = contract(mine, acts_ref[b], 1, 1)
        out_ref[:, columns] = (total[:, columns] + bias_ref[b : b + 1, :] - target).astype(BF16)


def own_error_of(offset, arrived, acts_out_t, dec_bias):
    return on_chip(
        error_kernel,
        "own_error",
        (offset, arrived, acts_out_t, dec_bias),
        jax.ShapeDtypeStruct(arrived.shape[1:], BF16),
    )


def upstream_rows(layers, error_ref, weight_ref, store):
    width, feature_dev = weight_ref.shape[1:]
    for a in range(layers):
        total = None
        for b in range(a, layers):
            term = contract(
                error_ref[:, b * width : (b + 1) * width], weight_ref[pair_number(a, b, layers)], 1, 0
            )
            total = term if total is None else total + term
        store(total.astype(BF16), a * feature_dev // LANES)


def upstream_ours_kernel(layers, ours_ref, weight_ref, out_ref):
    blocks = out_ref.shape[0]
    upstream_rows(layers, ours_ref, weight_ref, lambda x, first: store_tiles(out_ref, x, first, blocks))


def upstream_ours(ours, dec_t, layers, blocks):
    half = ours.shape[0]
    rows = half // blocks * layers * dec_t.shape[2] // LANES
    return on_chip(
        functools.partial(upstream_ours_kernel, layers),
        "upstream_ours",
        (ours, dec_t),
        jax.ShapeDtypeStruct((blocks, rows, LANES), BF16),
        2 * half * dec_t.size,
    )


def decoder_grads(layers, error_ref, features_ref, held_ref, out_hbm, sems):
    width, feature_dev = held_ref.shape[1:]
    copies = []
    for a in range(layers):
        for b in range(a, layers):
            pair = pair_number(a, b, layers)
            held_ref[pair] = contract(
                error_ref[:, b * width : (b + 1) * width],
                features_ref[:, a * feature_dev : (a + 1) * feature_dev],
                0,
                0,
            )
            copy = pltpu.make_async_copy(held_ref.at[pair], out_hbm.at[pair], sems.at[pair])
            copy.start()
            copies.append(copy)
    return copies


def upstream_kernel(
    layers, core_ref, ours_ref, theirs_ref, sent_ref, weight_ref, features_ref,
    out_ref, error_ref, grad_hbm, held_ref, sems,
):
    blocks, rows, _ = sent_ref.shape
    half = ours_ref.shape[0]
    core = core_ref[0]
    for ref, side in ((ours_ref, core), (theirs_ref, 1 - core)):
        error_ref[pl.ds(pl.multiple_of(side * half, half), half), :] = ref[...]
    for k in range(blocks):
        out_ref[core * blocks + k, :rows, :] = sent_ref[k]
    other = out_ref.at[pl.ds((1 - core) * blocks, blocks)]
    upstream_rows(layers, theirs_ref, weight_ref, lambda x, first: store_tiles(other, x, first, blocks))
    wide = error_ref[...].astype(F32)
    squared = jnp.sum(wide * wide)
    coarse = squared.astype(BF16).astype(F32)
    fine = squared - coarse
    lane = lax.broadcasted_iota(jnp.int32, (EXTRA, LANES), 1)
    extra = jnp.where(lane == 0, coarse, jnp.where(lane == 1, fine, 0.0)).astype(BF16)
    for k in range(2 * blocks):
        out_ref[k, rows:, :] = extra

    @pl.when(core == EARLY)
    def _():
        for copy in decoder_grads(layers, error_ref, features_ref, held_ref, grad_hbm, sems):
            copy.wait()


def upstream(core, ours, theirs, sent_ours, dec_t, features, layers):
    half, columns = ours.shape
    blocks = sent_ours.shape[0]
    vmem = pl.BlockSpec(memory_space=pltpu.VMEM)
    sent = sent_shape(2 * blocks, 2 * half, layers * dec_t.shape[2])
    return pl.pallas_call(
        functools.partial(upstream_kernel, layers),
        in_specs=[pl.BlockSpec(memory_space=pltpu.SMEM)] + [vmem] * 5,
        out_specs=[vmem, vmem, pl.BlockSpec(memory_space=pl.ANY)],
        out_shape=[
            pltpu.VMEM(sent.shape, BF16),
            pltpu.VMEM((2 * half, columns), BF16),
            jax.ShapeDtypeStruct(dec_t.shape, F32),
        ],
        scratch_shapes=[pltpu.VMEM(dec_t.shape, F32), pltpu.SemaphoreType.DMA((dec_t.shape[0],))],
        compiler_params=pltpu.CompilerParams(vmem_limit_bytes=VMEM),
        name="upstream",
    )(core, ours, theirs, sent_ours, dec_t, features)


def delta_kernel(arrived_ref, features_ref, own_ref, extra_ref):
    slots = arrived_ref.shape[0]
    rows, columns = features_ref.shape
    total = arrived_ref[0].astype(F32)
    for k in range(1, slots):
        total = total + arrived_ref[k].astype(F32)
    for j in range(columns // LANES):
        at = slice(j * LANES, (j + 1) * LANES)
        delta = jnp.where(features_ref[:, at] > 0, total[j * rows : (j + 1) * rows, :], 0.0)
        own_ref[:, at] = delta.astype(BF16)
    last = columns // LANES * rows
    extra_ref[...] = total[last : last + EXTRA, :]


def own_delta_of(arrived, own_features):
    return on_chip(
        delta_kernel,
        "own_delta",
        (arrived, own_features),
        [pltpu.VMEM(own_features.shape, BF16), pltpu.VMEM((EXTRA, LANES), F32)],
    )


def gradients_kernel(
    share, core_ref, acts_ref, delta_ref, features_ref, error_ref, extra_ref, early_hbm,
    enc_hbm, bias_hbm, dec_hbm, mse_hbm,
    enc_held, bias_held, dec_held, mse_held, enc_sems, dec_sems, small_sems,
):
    del early_hbm
    layers, _, tokens = acts_ref.shape
    feature_dev = enc_held.shape[2]
    late = core_ref[0] != EARLY
    leaving = []

    def send(held, out, sem):
        copy = pltpu.make_async_copy(held, out, sem)
        copy.start()
        leaving.append(copy)

    def layer(a):
        return slice(a * feature_dev, (a + 1) * feature_dev)

    @pl.when(late)
    def _():
        decoder_grads(layers, error_ref, features_ref, dec_held, dec_hbm, dec_sems)

    mse_held[...] = jnp.sum(extra_ref[:1, :], axis=1, keepdims=True) * share
    send(mse_held, mse_hbm, small_sems.at[0])
    ones = jnp.ones((8, tokens), BF16)
    for a in range(layers):
        bias_held[a : a + 1, :] = contract(ones, delta_ref[:, layer(a)], 1, 0)[:1]
    send(bias_held, bias_hbm, small_sems.at[1])
    for a in range(layers):
        enc_held[a] = contract(acts_ref[a], delta_ref[:, layer(a)], 1, 0)
        send(enc_held.at[a], enc_hbm.at[a], enc_sems.at[a])
    for copy in leaving:
        copy.wait()

    @pl.when(late)
    def _():
        for pair in range(dec_held.shape[0]):
            pltpu.make_async_copy(dec_held.at[pair], dec_hbm.at[pair], dec_sems.at[pair]).wait()


def gradients(core, acts_t, delta, features, error, extra, dec_grad_t, share):
    layers, width, _ = acts_t.shape
    feature_dev = delta.shape[1] // layers
    pairs = layers * (layers + 1) // 2
    vmem = pl.BlockSpec(memory_space=pltpu.VMEM)
    anywhere = pl.BlockSpec(memory_space=pl.ANY)
    shapes = (
        (layers, width, feature_dev),
        (layers, feature_dev),
        (pairs, width, feature_dev),
        (1, 1),
    )
    return pl.pallas_call(
        functools.partial(gradients_kernel, share),
        in_specs=[pl.BlockSpec(memory_space=pltpu.SMEM)] + [vmem] * 5 + [anywhere],
        out_specs=[anywhere] * 4,
        out_shape=[jax.ShapeDtypeStruct(shape, F32) for shape in shapes],
        scratch_shapes=[pltpu.VMEM(shape, F32) for shape in shapes]
        + [pltpu.SemaphoreType.DMA((count,)) for count in (layers, pairs, 2)],
        input_output_aliases={6: 2},
        compiler_params=pltpu.CompilerParams(vmem_limit_bytes=VMEM),
        name="gradients",
    )(core, acts_t, delta, features, error, extra, dec_grad_t)


def local(acts_in, acts_out, enc_weight, enc_bias, dec_weight, dec_bias):
    layers, tokens, _ = acts_in.shape
    slots = lax.axis_size(SLOT)
    chips = lax.axis_size(CHIPS)
    core = lax.axis_index(CORE)
    acts_t = jnp.transpose(acts_in, (0, 2, 1))
    dec_t = jnp.transpose(dec_weight, (0, 2, 1))

    half = tokens // 2
    portion = half // chips
    core = core.reshape(1)
    offset = core * half + lax.axis_index(CHIPS) * portion
    sent = encode(acts_t, enc_weight, slots)
    sent, core, offset = lax.optimization_barrier((sent, core, offset))
    own_features = own_features_of(exchange(sent, SLOT), enc_bias, tokens // slots)
    features = sent_to_all(own_features, SLOT).reshape(tokens, -1)

    swap = [(0, 1), (1, 0)]
    from_core = lax.ppermute(decode(core, features, dec_t, layers, False), CORE, swap)
    chip_sum = (decode(core, features, dec_t, layers, True) + from_core.astype(F32)).astype(BF16)
    arrived = exchange(chip_sum.reshape(chips, portion, -1), CHIPS)
    own_error = own_error_of(offset, arrived, jnp.transpose(acts_out, (0, 2, 1)), dec_bias)
    half_error = sent_to_all(own_error, CHIPS).reshape(half, -1)
    other_error = lax.ppermute(half_error, CORE, swap)
    sent_ours = upstream_ours(half_error, dec_t, layers, slots // 2)
    sent, error, early = upstream(core, half_error, other_error, sent_ours, dec_t, features, layers)
    own_delta, extra = own_delta_of(exchange(sent, SLOT), own_features)
    delta = sent_to_all(own_delta, SLOT).reshape(tokens, -1)
    share = 1.0 / (layers * tokens * D)
    enc_grad, bias_grad, dec_grad_t, mse = gradients(
        core, acts_t, delta, features, error, extra, early, share
    )
    return (enc_grad, bias_grad, jnp.transpose(dec_grad_t, (0, 2, 1)), mse.reshape(()))


def solution(mesh):
    split = Mesh(mesh.devices.reshape(2, 4, 2, 8, 2), (*SLOT, *FEAT))
    in_specs = (
        P(None, None, SLOT),
        P(None, None, SLOT),
        P(None, SLOT, FEAT),
        P(None, FEAT),
        P(None, FEAT, SLOT),
        P(None, SLOT),
    )
    out_specs = (P(None, SLOT, FEAT), P(None, FEAT), P(None, FEAT, SLOT), P())
    return jax.shard_map(local, mesh=split, in_specs=in_specs, out_specs=out_specs, check_vma=False)
```

```python
import functools

import jax
import jax.numpy as jnp
from jax import lax
from jax.experimental import pallas as pl
from jax.experimental.pallas import tpu as pltpu
from jax.sharding import Mesh
from jax.sharding import PartitionSpec as P

D = 2304
SLOT = ("slot_0", "slot_1")
FEAT = ("feat_0", "feat_1", "feat_2")
CHIPS = ("feat_0", "feat_1")
CORE = "feat_2"
LANES = 128
EXTRA = 16
VMEM = 16 * 2**20
ALONE = 56 * 2**20
OCTAVES = 250.0
ABOVE = 1.0078125
TINY = 1e-30
LEAST = 1e-12
F32 = jnp.float32
BF16 = jnp.bfloat16


def exchange(tiles, axis):
    return lax.all_to_all(tiles, axis, split_axis=0, concat_axis=0, tiled=True)


def sent_to_all(x, axis):
    return exchange(jnp.broadcast_to(x[None], (lax.axis_size(axis), *x.shape)), axis)


def pair_number(a, b, layers):
    return a * layers - a * (a - 1) // 2 + (b - a)


def contract(x, y, x_dim, y_dim):
    return lax.dot_general(x, y, (((x_dim,), (y_dim,)), ((), ())), preferred_element_type=F32)


def store_tiles(out_ref, value, first, slots):
    rows = value.shape[0] // slots
    for k in range(slots):
        for j in range(value.shape[1] // LANES):
            out_ref[k, (first + j) * rows : (first + j + 1) * rows, :] = value[
                k * rows : (k + 1) * rows, j * LANES : (j + 1) * LANES
            ]


def encode_kernel(acts_hbm, weight_hbm, out_ref, acts_ref, weight_ref, acts_sems, weight_sems):
    layers = acts_ref.shape[0]
    arriving = []
    for a in range(layers):
        for source, held, sems in ((weight_hbm, weight_ref, weight_sems), (acts_hbm, acts_ref, acts_sems)):
            copy = pltpu.make_async_copy(source.at[a], held.at[a], sems.at[a])
            copy.start()
            arriving.append(copy)
    feature_dev = weight_ref.shape[2]
    slots = out_ref.shape[0]
    rows = acts_ref.shape[2] // slots
    tiles = feature_dev // LANES
    scales = []
    for a in range(layers):
        arriving[2 * a].wait()
        arriving[2 * a + 1].wait()
        preact = contract(acts_ref[a], weight_ref[a], 0, 0)
        size = jnp.abs(preact)
        largest = jnp.maximum(jnp.max(size, axis=1, keepdims=True), TINY)
        scale = (largest * ABOVE).astype(BF16).astype(F32)
        square = jnp.maximum(size * (1.0 / scale), LEAST)
        code = jnp.exp2(square * lax.rsqrt(square) * OCTAVES - OCTAVES / 2)
        store_tiles(out_ref, jnp.where(preact < 0, -code, code).astype(BF16), a * tiles, slots)
        scales.append(scale)
    lane = lax.broadcasted_iota(jnp.int32, (EXTRA, LANES), 1)
    for k in range(slots):
        extra = jnp.zeros((EXTRA, LANES), F32)
        for part in range(rows // EXTRA):
            at = k * rows + part * EXTRA
            for a in range(layers):
                extra = jnp.where(lane == part * layers + a, scales[a][at : at + EXTRA], extra)
        out_ref[k, layers * tiles * rows :, :] = extra.astype(BF16)


def on_chip(kernel, name, args, out_shape, scratch_shapes=()):
    vmem = pl.BlockSpec(memory_space=pltpu.VMEM)
    smem = pl.BlockSpec(memory_space=pltpu.SMEM)
    return pl.pallas_call(
        kernel,
        in_specs=[smem if arg.dtype == jnp.int32 else vmem for arg in args],
        out_specs=jax.tree.map(lambda _: vmem, out_shape),
        out_shape=out_shape,
        compiler_params=pltpu.CompilerParams(vmem_limit_bytes=VMEM),
        scratch_shapes=scratch_shapes,
        name=name,
    )(*args)


def sent_shape(slots, tokens, columns):
    return jax.ShapeDtypeStruct((slots, tokens // slots * columns // LANES + EXTRA, LANES), BF16)


def encode(acts_t, enc_weight, slots):
    layers, _, tokens = acts_t.shape
    shape = sent_shape(slots, tokens, layers * enc_weight.shape[2])
    anywhere = pl.BlockSpec(memory_space=pl.ANY)
    return pl.pallas_call(
        encode_kernel,
        in_specs=[anywhere, anywhere],
        out_specs=pl.BlockSpec(memory_space=pltpu.VMEM),
        out_shape=pltpu.VMEM(shape.shape, shape.dtype),
        scratch_shapes=[
            pltpu.VMEM(acts_t.shape, BF16),
            pltpu.VMEM(enc_weight.shape, BF16),
            pltpu.SemaphoreType.DMA((layers,)),
            pltpu.SemaphoreType.DMA((layers,)),
        ],
        compiler_params=pltpu.CompilerParams(vmem_limit_bytes=ALONE),
        name="encode",
    )(acts_t, enc_weight)


def features_kernel(arrived_ref, bias_ref, own_ref):
    slots = arrived_ref.shape[0]
    rows = own_ref.shape[0]
    layers, feature_dev = bias_ref.shape
    tiles = feature_dev // LANES
    scales = []
    for k in range(slots):
        extra = arrived_ref[k, layers * tiles * rows :, :].astype(F32)
        parts = rows // EXTRA
        scales.append(
            [
                jnp.concatenate([extra[:, p * layers + a : p * layers + a + 1] for p in range(parts)], axis=0)
                for a in range(layers)
            ]
        )
    for a in range(layers):
        for j in range(tiles):
            at = (a * tiles + j) * rows
            columns = slice(j * LANES, (j + 1) * LANES)
            total = jnp.broadcast_to(bias_ref[a : a + 1, columns], (rows, LANES))
            for k in range(slots):
                code = arrived_ref[k, at : at + rows, :].astype(F32)
                root = jnp.log2(jnp.abs(code)) * (1.0 / OCTAVES) + 0.5
                size = root * root * scales[k][a]
                total = total + jnp.where(code < 0, -size, size)
            at = (a * tiles + j) * LANES
            own_ref[:, at : at + LANES] = jnp.maximum(total, 0.0).astype(BF16)


def own_features_of(arrived, enc_bias, rows):
    shape = (rows, enc_bias.size)
    return on_chip(
        features_kernel, "own_features", (arrived, enc_bias), jax.ShapeDtypeStruct(shape, BF16)
    )


def decode_kernel(layers, core_ref, features_ref, weight_ref, theirs_ref, ours_ref, held_ref):
    width, feature_dev = weight_ref.shape[1:]
    chips, cores, rows, _ = held_ref.shape
    core = core_ref[0]
    for b in range(layers):
        total = None
        for a in range(b + 1):
            term = contract(
                features_ref[:, a * feature_dev : (a + 1) * feature_dev],
                weight_ref[pair_number(a, b, layers)],
                1,
                1,
            )
            total = term if total is None else total + term
        held_ref[:, :, :, b * width : (b + 1) * width] = total.reshape(chips, cores, rows, width)
    for ref, side in ((theirs_ref, 1 - core), (ours_ref, core)):
        ref[...] = held_ref[:, side].reshape(ref.shape).astype(ref.dtype)


def decode(core, features, dec_t, layers, chips):
    tokens = features.shape[0]
    columns = layers * dec_t.shape[1]
    return on_chip(
        functools.partial(decode_kernel, layers),
        "decode",
        (core, features, dec_t),
        [jax.ShapeDtypeStruct((tokens // 2, columns), kind) for kind in (BF16, F32)],
        [pltpu.VMEM((chips, 2, tokens // chips // 2, columns), F32)],
    )


def error_kernel(offset_ref, arrived_ref, acts_ref, bias_ref, out_ref):
    chips, rows, _ = arrived_ref.shape
    layers, width, tokens = acts_ref.shape
    row = lax.broadcasted_iota(jnp.int32, (rows, tokens), 0)
    token = lax.broadcasted_iota(jnp.int32, (rows, tokens), 1)
    mine = jnp.where(token == row + offset_ref[0], 1.0, 0.0).astype(BF16)
    total = arrived_ref[0].astype(F32)
    for k in range(1, chips):
        total = total + arrived_ref[k].astype(F32)
    for b in range(layers):
        columns = slice(b * width, (b + 1) * width)
        target = contract(mine, acts_ref[b], 1, 1)
        out_ref[:, columns] = (total[:, columns] + bias_ref[b : b + 1, :] - target).astype(BF16)


def own_error_of(offset, arrived, acts_out_t, dec_bias):
    return on_chip(
        error_kernel,
        "own_error",
        (offset, arrived, acts_out_t, dec_bias),
        jax.ShapeDtypeStruct(arrived.shape[1:], BF16),
    )


def upstream_kernel(layers, error_ref, weight_ref, out_ref):
    width, feature_dev = weight_ref.shape[1:]
    slots = out_ref.shape[0]
    for a in range(layers):
        total = None
        for b in range(a, layers):
            term = contract(
                error_ref[:, b * width : (b + 1) * width], weight_ref[pair_number(a, b, layers)], 1, 0
            )
            total = term if total is None else total + term
        store_tiles(out_ref, total.astype(BF16), a * feature_dev // LANES, slots)
    wide = error_ref[...].astype(F32)
    squared = jnp.sum(wide * wide)
    coarse = squared.astype(BF16).astype(F32)
    fine = squared - coarse
    lane = lax.broadcasted_iota(jnp.int32, (EXTRA, LANES), 1)
    extra = jnp.where(lane == 0, coarse, jnp.where(lane == 1, fine, 0.0)).astype(BF16)
    for k in range(slots):
        out_ref[k, out_ref.shape[1] - EXTRA :, :] = extra


def upstream(error, dec_t, layers, slots):
    return on_chip(
        functools.partial(upstream_kernel, layers),
        "upstream",
        (error, dec_t),
        sent_shape(slots, error.shape[0], layers * dec_t.shape[2]),
    )


def delta_kernel(arrived_ref, features_ref, own_ref, extra_ref):
    slots = arrived_ref.shape[0]
    rows, columns = features_ref.shape
    total = arrived_ref[0].astype(F32)
    for k in range(1, slots):
        total = total + arrived_ref[k].astype(F32)
    for j in range(columns // LANES):
        at = slice(j * LANES, (j + 1) * LANES)
        delta = jnp.where(features_ref[:, at] > 0, total[j * rows : (j + 1) * rows, :], 0.0)
        own_ref[:, at] = delta.astype(BF16)
    last = columns // LANES * rows
    extra_ref[...] = total[last : last + EXTRA, :]


def own_delta_of(arrived, own_features):
    return on_chip(
        delta_kernel,
        "own_delta",
        (arrived, own_features),
        [pltpu.VMEM(own_features.shape, BF16), pltpu.VMEM((EXTRA, LANES), F32)],
    )


def gradients_kernel(
    share, acts_ref, delta_ref, features_ref, error_ref, extra_ref,
    enc_hbm, bias_hbm, dec_hbm, mse_hbm,
    enc_held, bias_held, dec_held, mse_held, enc_sems, dec_sems, small_sems,
):
    layers, width, tokens = acts_ref.shape
    feature_dev = enc_held.shape[2]
    leaving = []

    def send(held, out, sem):
        copy = pltpu.make_async_copy(held, out, sem)
        copy.start()
        leaving.append(copy)

    def layer(a):
        return slice(a * feature_dev, (a + 1) * feature_dev)

    for a in range(layers):
        for b in range(a, layers):
            pair = pair_number(a, b, layers)
            dec_held[pair] = contract(
                error_ref[:, b * width : (b + 1) * width], features_ref[:, layer(a)], 0, 0
            )
            send(dec_held.at[pair], dec_hbm.at[pair], dec_sems.at[pair])
    mse_held[...] = jnp.sum(extra_ref[:1, :], axis=1, keepdims=True) * share
    send(mse_held, mse_hbm, small_sems.at[0])
    ones = jnp.ones((8, tokens), BF16)
    for a in range(layers):
        bias_held[a : a + 1, :] = contract(ones, delta_ref[:, layer(a)], 1, 0)[:1]
    send(bias_held, bias_hbm, small_sems.at[1])
    for a in range(layers):
        enc_held[a] = contract(acts_ref[a], delta_ref[:, layer(a)], 1, 0)
        send(enc_held.at[a], enc_hbm.at[a], enc_sems.at[a])
    for copy in leaving:
        copy.wait()


def gradients(acts_t, delta, features, error, extra, share):
    layers, width, _ = acts_t.shape
    feature_dev = delta.shape[1] // layers
    pairs = layers * (layers + 1) // 2
    vmem = pl.BlockSpec(memory_space=pltpu.VMEM)
    anywhere = pl.BlockSpec(memory_space=pl.ANY)
    shapes = (
        (layers, width, feature_dev),
        (layers, feature_dev),
        (pairs, width, feature_dev),
        (1, 1),
    )
    return pl.pallas_call(
        functools.partial(gradients_kernel, share),
        in_specs=[vmem] * 5,
        out_specs=[anywhere] * 4,
        out_shape=[jax.ShapeDtypeStruct(shape, F32) for shape in shapes],
        scratch_shapes=[pltpu.VMEM(shape, F32) for shape in shapes]
        + [pltpu.SemaphoreType.DMA((count,)) for count in (layers, pairs, 2)],
        compiler_params=pltpu.CompilerParams(vmem_limit_bytes=VMEM),
        name="gradients",
    )(acts_t, delta, features, error, extra)


def local(acts_in, acts_out, enc_weight, enc_bias, dec_weight, dec_bias):
    layers, tokens, _ = acts_in.shape
    slots = lax.axis_size(SLOT)
    chips = lax.axis_size(CHIPS)
    core = lax.axis_index(CORE)
    acts_t = jnp.transpose(acts_in, (0, 2, 1))
    dec_t = jnp.transpose(dec_weight, (0, 2, 1))

    portion = tokens // chips // 2
    core = core.reshape(1)
    offset = (lax.axis_index(CHIPS) * 2 + core) * portion
    sent = encode(acts_t, enc_weight, slots)
    sent, core, offset = lax.optimization_barrier((sent, core, offset))
    own_features = own_features_of(exchange(sent, SLOT), enc_bias, tokens // slots)
    features = sent_to_all(own_features, SLOT).reshape(tokens, -1)

    swap = [(0, 1), (1, 0)]
    theirs, ours = decode(core, features, dec_t, layers, chips)
    chip_sum = (ours + lax.ppermute(theirs, CORE, swap).astype(F32)).astype(BF16)
    arrived = exchange(chip_sum.reshape(chips, portion, -1), CHIPS)
    own_error = own_error_of(offset, arrived, jnp.transpose(acts_out, (0, 2, 1)), dec_bias)
    other_error = lax.ppermute(own_error, CORE, swap)
    first = core[0] == 0
    chip_error = jnp.concatenate(
        [jnp.where(first, own_error, other_error), jnp.where(first, other_error, own_error)], axis=0
    )
    error = sent_to_all(chip_error, CHIPS).reshape(tokens, -1)

    sent = upstream(error, dec_t, layers, slots)
    own_delta, extra = own_delta_of(exchange(sent, SLOT), own_features)
    delta = sent_to_all(own_delta, SLOT).reshape(tokens, -1)
    share = 1.0 / (layers * tokens * D)
    enc_grad, bias_grad, dec_grad_t, mse = gradients(acts_t, delta, features, error, extra, share)
    return (enc_grad, bias_grad, jnp.transpose(dec_grad_t, (0, 2, 1)), mse.reshape(()))


def solution(mesh):
    split = Mesh(mesh.devices.reshape(2, 4, 2, 8, 2), (*SLOT, *FEAT))
    in_specs = (
        P(None, None, SLOT),
        P(None, None, SLOT),
        P(None, SLOT, FEAT),
        P(None, FEAT),
        P(None, FEAT, SLOT),
        P(None, SLOT),
    )
    out_specs = (P(None, SLOT, FEAT), P(None, FEAT), P(None, FEAT, SLOT), P())
    return jax.shard_map(local, mesh=split, in_specs=in_specs, out_specs=out_specs, check_vma=False)
```

```python
import functools

import jax
import jax.numpy as jnp
from jax import lax
from jax.experimental import pallas as pl
from jax.experimental.pallas import tpu as pltpu
from jax.sharding import Mesh
from jax.sharding import PartitionSpec as P

D = 2304
SLOT = ("slot_0", "slot_1")
FEAT = ("feat_0", "feat_1", "feat_2")
CHIPS = ("feat_0", "feat_1")
CORE = "feat_2"
LANES = 128
EXTRA = 16
VMEM = 16 * 2**20
ALONE = 56 * 2**20
OCTAVES = 250.0
ABOVE = 1.0078125
TINY = 1e-30
LEAST = 1e-12
F32 = jnp.float32
BF16 = jnp.bfloat16


def exchange(tiles, axis):
    return lax.all_to_all(tiles, axis, split_axis=0, concat_axis=0, tiled=True)


def sent_to_all(x, axis):
    return exchange(jnp.broadcast_to(x[None], (lax.axis_size(axis), *x.shape)), axis)


def pair_number(a, b, layers):
    return a * layers - a * (a - 1) // 2 + (b - a)


def contract(x, y, x_dim, y_dim):
    return lax.dot_general(x, y, (((x_dim,), (y_dim,)), ((), ())), preferred_element_type=F32)


def store_tiles(out_ref, value, first, slots):
    rows = value.shape[0] // slots
    for k in range(slots):
        for j in range(value.shape[1] // LANES):
            out_ref[k, (first + j) * rows : (first + j + 1) * rows, :] = value[
                k * rows : (k + 1) * rows, j * LANES : (j + 1) * LANES
            ]


def encode_kernel(acts_hbm, weight_hbm, out_ref, acts_ref, weight_ref, acts_sems, weight_sems):
    layers = acts_ref.shape[0]
    arriving = []
    for a in range(layers):
        for source, held, sems in ((weight_hbm, weight_ref, weight_sems), (acts_hbm, acts_ref, acts_sems)):
            copy = pltpu.make_async_copy(source.at[a], held.at[a], sems.at[a])
            copy.start()
            arriving.append(copy)
    feature_dev = weight_ref.shape[2]
    slots = out_ref.shape[0]
    rows = acts_ref.shape[2] // slots
    tiles = feature_dev // LANES
    scales = []
    for a in range(layers):
        arriving[2 * a].wait()
        arriving[2 * a + 1].wait()
        preact = contract(acts_ref[a], weight_ref[a], 0, 0)
        size = jnp.abs(preact)
        largest = jnp.maximum(jnp.max(size, axis=1, keepdims=True), TINY)
        scale = (largest * ABOVE).astype(BF16).astype(F32)
        square = jnp.maximum(size * (1.0 / scale), LEAST)
        code = jnp.exp2(square * lax.rsqrt(square) * OCTAVES - OCTAVES / 2)
        store_tiles(out_ref, jnp.where(preact < 0, -code, code).astype(BF16), a * tiles, slots)
        scales.append(scale)
    lane = lax.broadcasted_iota(jnp.int32, (EXTRA, LANES), 1)
    for k in range(slots):
        extra = jnp.zeros((EXTRA, LANES), F32)
        for part in range(rows // EXTRA):
            at = k * rows + part * EXTRA
            for a in range(layers):
                extra = jnp.where(lane == part * layers + a, scales[a][at : at + EXTRA], extra)
        out_ref[k, layers * tiles * rows :, :] = extra.astype(BF16)


def on_chip(kernel, name, args, out_shape, flops=None):
    vmem = pl.BlockSpec(memory_space=pltpu.VMEM)
    smem = pl.BlockSpec(memory_space=pltpu.SMEM)
    return pl.pallas_call(
        kernel,
        in_specs=[smem if arg.dtype == jnp.int32 else vmem for arg in args],
        out_specs=jax.tree.map(lambda _: vmem, out_shape),
        out_shape=out_shape,
        compiler_params=pltpu.CompilerParams(vmem_limit_bytes=VMEM),
        cost_estimate=flops and pl.CostEstimate(flops=flops, bytes_accessed=flops // 128, transcendentals=0),
        name=name,
    )(*args)


def sent_shape(slots, tokens, columns):
    return jax.ShapeDtypeStruct((slots, tokens // slots * columns // LANES + EXTRA, LANES), BF16)


def encode(acts_t, enc_weight, slots):
    layers, _, tokens = acts_t.shape
    shape = sent_shape(slots, tokens, layers * enc_weight.shape[2])
    anywhere = pl.BlockSpec(memory_space=pl.ANY)
    return pl.pallas_call(
        encode_kernel,
        in_specs=[anywhere, anywhere],
        out_specs=pl.BlockSpec(memory_space=pltpu.VMEM),
        out_shape=pltpu.VMEM(shape.shape, shape.dtype),
        scratch_shapes=[
            pltpu.VMEM(acts_t.shape, BF16),
            pltpu.VMEM(enc_weight.shape, BF16),
            pltpu.SemaphoreType.DMA((layers,)),
            pltpu.SemaphoreType.DMA((layers,)),
        ],
        compiler_params=pltpu.CompilerParams(vmem_limit_bytes=ALONE),
        name="encode",
    )(acts_t, enc_weight)


def features_kernel(arrived_ref, bias_ref, own_ref):
    slots = arrived_ref.shape[0]
    rows = own_ref.shape[0]
    layers, feature_dev = bias_ref.shape
    tiles = feature_dev // LANES
    scales = []
    for k in range(slots):
        extra = arrived_ref[k, layers * tiles * rows :, :].astype(F32)
        parts = rows // EXTRA
        scales.append(
            [
                jnp.concatenate([extra[:, p * layers + a : p * layers + a + 1] for p in range(parts)], axis=0)
                for a in range(layers)
            ]
        )
    for a in range(layers):
        for j in range(tiles):
            at = (a * tiles + j) * rows
            columns = slice(j * LANES, (j + 1) * LANES)
            total = jnp.broadcast_to(bias_ref[a : a + 1, columns], (rows, LANES))
            for k in range(slots):
                code = arrived_ref[k, at : at + rows, :].astype(F32)
                root = jnp.log2(jnp.abs(code)) * (1.0 / OCTAVES) + 0.5
                size = root * root * scales[k][a]
                total = total + jnp.where(code < 0, -size, size)
            at = (a * tiles + j) * LANES
            own_ref[:, at : at + LANES] = jnp.maximum(total, 0.0).astype(BF16)


def own_features_of(arrived, enc_bias, rows):
    shape = (rows, enc_bias.size)
    return on_chip(
        features_kernel, "own_features", (arrived, enc_bias), jax.ShapeDtypeStruct(shape, BF16)
    )


def decode_kernel(layers, ours, core_ref, features_ref, weight_ref, out_ref):
    width, feature_dev = weight_ref.shape[1:]
    half = out_ref.shape[0]
    side = core_ref[0] if ours else 1 - core_ref[0]
    rows = pl.ds(pl.multiple_of(side * half, half), half)
    for b in range(layers):
        total = None
        for a in range(b + 1):
            term = contract(
                features_ref[rows, a * feature_dev : (a + 1) * feature_dev],
                weight_ref[pair_number(a, b, layers)],
                1,
                1,
            )
            total = term if total is None else total + term
        out_ref[:, b * width : (b + 1) * width] = total.astype(out_ref.dtype)


def decode(core, features, dec_t, layers, ours):
    half = features.shape[0] // 2
    return on_chip(
        functools.partial(decode_kernel, layers, ours),
        "decode_ours" if ours else "decode_theirs",
        (core, features, dec_t),
        jax.ShapeDtypeStruct((half, layers * dec_t.shape[1]), F32 if ours else BF16),
        2 * half * dec_t.size,
    )


def error_kernel(offset_ref, arrived_ref, acts_ref, bias_ref, out_ref):
    chips, rows, _ = arrived_ref.shape
    layers, width, tokens = acts_ref.shape
    row = lax.broadcasted_iota(jnp.int32, (rows, tokens), 0)
    token = lax.broadcasted_iota(jnp.int32, (rows, tokens), 1)
    mine = jnp.where(token == row + offset_ref[0], 1.0, 0.0).astype(BF16)
    total = arrived_ref[0].astype(F32)
    for k in range(1, chips):
        total = total + arrived_ref[k].astype(F32)
    for b in range(layers):
        columns = slice(b * width, (b + 1) * width)
        target = contract(mine, acts_ref[b], 1, 1)
        out_ref[:, columns] = (total[:, columns] + bias_ref[b : b + 1, :] - target).astype(BF16)


def own_error_of(offset, arrived, acts_out_t, dec_bias):
    return on_chip(
        error_kernel,
        "own_error",
        (offset, arrived, acts_out_t, dec_bias),
        jax.ShapeDtypeStruct(arrived.shape[1:], BF16),
    )


def upstream_kernel(layers, error_ref, ours_ref, theirs_ref, out_ref):
    width, feature_dev = ours_ref.shape[1:]
    slots = out_ref.shape[0]
    tiles = feature_dev // LANES
    for side, weight_ref in enumerate((ours_ref, theirs_ref)):
        for a in range(layers):
            total = None
            for b in range(a, layers):
                term = contract(
                    error_ref[:, b * width : (b + 1) * width], weight_ref[pair_number(a, b, layers)], 1, 0
                )
                total = term if total is None else total + term
            store_tiles(out_ref, total.astype(BF16), (side * layers + a) * tiles, slots)
    wide = error_ref[...].astype(F32)
    squared = jnp.sum(wide * wide)
    coarse = squared.astype(BF16).astype(F32)
    fine = squared - coarse
    lane = lax.broadcasted_iota(jnp.int32, (EXTRA, LANES), 1)
    extra = jnp.where(lane == 0, coarse, jnp.where(lane == 1, fine, 0.0)).astype(BF16)
    for k in range(slots):
        out_ref[k, out_ref.shape[1] - EXTRA :, :] = extra


def upstream(error, dec_t, other_dec_t, layers, slots):
    return on_chip(
        functools.partial(upstream_kernel, layers),
        "upstream",
        (error, dec_t, other_dec_t),
        sent_shape(slots, error.shape[0], 2 * layers * dec_t.shape[2]),
    )


def delta_kernel(arrived_ref, ours_ref, theirs_ref, own_ref, extra_ref):
    slots = arrived_ref.shape[0]
    rows, columns = ours_ref.shape
    total = arrived_ref[0].astype(F32)
    for k in range(1, slots):
        total = total + arrived_ref[k].astype(F32)
    tiles = columns // LANES
    for side, features_ref in enumerate((ours_ref, theirs_ref)):
        for j in range(tiles):
            at = (side * tiles + j) * rows
            delta = jnp.where(
                features_ref[:, j * LANES : (j + 1) * LANES] > 0, total[at : at + rows, :], 0.0
            )
            own_ref[side, :, j * LANES : (j + 1) * LANES] = delta.astype(BF16)
    extra_ref[...] = total[2 * tiles * rows :, :]


def own_delta_of(arrived, ours, theirs):
    return on_chip(
        delta_kernel,
        "own_delta",
        (arrived, ours, theirs),
        [pltpu.VMEM((2, *ours.shape), BF16), pltpu.VMEM((EXTRA, LANES), F32)],
    )


def join(held_ref, core, ours_ref, theirs_ref):
    half = held_ref.shape[0] // 2
    for ref, side in ((ours_ref, core), (theirs_ref, 1 - core)):
        held_ref[pl.ds(pl.multiple_of(side * half, half), half), :] = ref[...].reshape(half, -1)


def decoder_grad_kernel(layers, core_ref, ours_ref, theirs_ref, features_ref, out_hbm, error_ref, held_ref, sems):
    width, feature_dev = held_ref.shape[1:]
    join(error_ref, core_ref[0], ours_ref, theirs_ref)
    leaving = []
    for a in range(layers):
        for b in range(a, layers):
            pair = pair_number(a, b, layers)
            held_ref[pair] = contract(
                error_ref[:, b * width : (b + 1) * width],
                features_ref[:, a * feature_dev : (a + 1) * feature_dev],
                0,
                0,
            )
            copy = pltpu.make_async_copy(held_ref.at[pair], out_hbm.at[pair], sems.at[pair])
            copy.start()
            leaving.append(copy)
    for copy in leaving:
        copy.wait()


def decoder_grad(core, ours, theirs, features, layers):
    tokens = features.shape[0]
    pairs = layers * (layers + 1) // 2
    shape = (pairs, ours.shape[1] // layers, features.shape[1] // layers)
    vmem = pl.BlockSpec(memory_space=pltpu.VMEM)
    return pl.pallas_call(
        functools.partial(decoder_grad_kernel, layers),
        in_specs=[pl.BlockSpec(memory_space=pltpu.SMEM)] + [vmem] * 3,
        out_specs=pl.BlockSpec(memory_space=pl.ANY),
        out_shape=jax.ShapeDtypeStruct(shape, F32),
        scratch_shapes=[
            pltpu.VMEM((tokens, ours.shape[1]), BF16),
            pltpu.VMEM(shape, F32),
            pltpu.SemaphoreType.DMA((pairs,)),
        ],
        compiler_params=pltpu.CompilerParams(vmem_limit_bytes=VMEM),
        cost_estimate=pl.CostEstimate(flops=2**29, bytes_accessed=2**22, transcendentals=0),
        name="decoder_grad",
    )(core, ours, theirs, features)


def encoder_grad_kernel(
    share, core_ref, acts_ref, ours_ref, theirs_ref, extra_ref, other_extra_ref,
    enc_hbm, bias_hbm, mse_hbm,
    enc_held, bias_held, mse_held, delta_ref, enc_sems, small_sems,
):
    layers, _, tokens = acts_ref.shape
    feature_dev = enc_held.shape[2]
    join(delta_ref, core_ref[0], ours_ref, theirs_ref)
    leaving = []

    def send(held, out, sem):
        copy = pltpu.make_async_copy(held, out, sem)
        copy.start()
        leaving.append(copy)

    def layer(a):
        return slice(a * feature_dev, (a + 1) * feature_dev)

    for a in range(layers):
        enc_held[a] = contract(acts_ref[a], delta_ref[:, layer(a)], 1, 0)
        send(enc_held.at[a], enc_hbm.at[a], enc_sems.at[a])
    both = extra_ref[:1, :] + other_extra_ref[:1, :]
    mse_held[...] = jnp.sum(both, axis=1, keepdims=True) * share
    send(mse_held, mse_hbm, small_sems.at[0])
    ones = jnp.ones((8, tokens), BF16)
    for a in range(layers):
        bias_held[a : a + 1, :] = contract(ones, delta_ref[:, layer(a)], 1, 0)[:1]
    send(bias_held, bias_hbm, small_sems.at[1])
    for copy in leaving:
        copy.wait()


def encoder_grad(core, acts_t, ours, theirs, extra, other_extra, share):
    layers, width, tokens = acts_t.shape
    columns = theirs.shape[1]
    vmem = pl.BlockSpec(memory_space=pltpu.VMEM)
    shapes = ((layers, width, columns // layers), (layers, columns // layers), (1, 1))
    return pl.pallas_call(
        functools.partial(encoder_grad_kernel, share),
        in_specs=[pl.BlockSpec(memory_space=pltpu.SMEM)] + [vmem] * 5,
        out_specs=[pl.BlockSpec(memory_space=pl.ANY)] * 3,
        out_shape=[jax.ShapeDtypeStruct(shape, F32) for shape in shapes],
        scratch_shapes=[pltpu.VMEM(shape, F32) for shape in shapes]
        + [pltpu.VMEM((tokens, columns), BF16)]
        + [pltpu.SemaphoreType.DMA((count,)) for count in (layers, 2)],
        compiler_params=pltpu.CompilerParams(vmem_limit_bytes=VMEM),
        name="encoder_grad",
    )(core, acts_t, ours, theirs, extra, other_extra)


def local(acts_in, acts_out, enc_weight, enc_bias, dec_weight, dec_bias):
    layers, tokens, _ = acts_in.shape
    slots = lax.axis_size(SLOT)
    chips = lax.axis_size(CHIPS)
    core = lax.axis_index(CORE)
    acts_t = jnp.transpose(acts_in, (0, 2, 1))
    dec_t = jnp.transpose(dec_weight, (0, 2, 1))

    half = tokens // 2
    portion = half // chips
    core = core.reshape(1)
    offset = core * half + lax.axis_index(CHIPS) * portion
    swap = [(0, 1), (1, 0)]
    other_dec_t = lax.ppermute(dec_t, CORE, swap)
    sent = encode(acts_t, enc_weight, slots)
    sent, core, offset = lax.optimization_barrier((sent, core, offset))
    arrived, other_dec_t = lax.optimization_barrier((exchange(sent, SLOT), other_dec_t))
    own_features = own_features_of(arrived, enc_bias, tokens // slots)
    features = sent_to_all(own_features, SLOT).reshape(tokens, -1)

    from_core = lax.ppermute(decode(core, features, dec_t, layers, False), CORE, swap)
    chip_sum = (decode(core, features, dec_t, layers, True) + from_core.astype(F32)).astype(BF16)
    rows = half // slots
    at = lax.axis_index(SLOT) * rows

    def block(side):
        return lax.dynamic_slice_in_dim(features, side * half + at, rows, 0)

    own_block = block(core[0])
    other_block = lax.ppermute(block(1 - core[0]), CORE, swap)
    chip_sum, own_block, other_block = lax.optimization_barrier((chip_sum, own_block, other_block))
    arrived = exchange(chip_sum.reshape(chips, portion, -1), CHIPS)
    own_error = own_error_of(offset, arrived, jnp.transpose(acts_out, (0, 2, 1)), dec_bias)
    half_error = sent_to_all(own_error, CHIPS).reshape(half, -1)
    other_error = lax.ppermute(half_error, CORE, swap)
    sent = upstream(half_error, dec_t, other_dec_t, layers, slots)
    own_delta, extra = own_delta_of(exchange(sent, SLOT), own_block, other_block)
    other_extra = lax.ppermute(extra, CORE, swap)
    gathered = sent_to_all(own_delta, SLOT)
    ours = gathered[:, 0].reshape(half, -1)
    theirs = lax.ppermute(gathered[:, 1].reshape(half, -1), CORE, swap)
    dec_grad_t = decoder_grad(core, half_error, other_error, features, layers)
    share = 1.0 / (layers * tokens * D)
    enc_grad, bias_grad, mse = encoder_grad(core, acts_t, ours, theirs, extra, other_extra, share)
    return (enc_grad, bias_grad, jnp.transpose(dec_grad_t, (0, 2, 1)), mse.reshape(()))


def solution(mesh):
    split = Mesh(mesh.devices.reshape(2, 4, 2, 8, 2), (*SLOT, *FEAT))
    in_specs = (
        P(None, None, SLOT),
        P(None, None, SLOT),
        P(None, SLOT, FEAT),
        P(None, FEAT),
        P(None, FEAT, SLOT),
        P(None, SLOT),
    )
    out_specs = (P(None, SLOT, FEAT), P(None, FEAT), P(None, FEAT, SLOT), P())
    return jax.shard_map(local, mesh=split, in_specs=in_specs, out_specs=out_specs, check_vma=False)
```
